32 devices in a mesh: dp: 8 (over z, core), seq: 4 (over y, x).
Axes of the slice: x: 2, y: 2, z: 4, core: 2. Of those that a mesh axis runs over, the one named last changes fastest.
Arguments:
- queries: bfloat16 [4096, 4096], P(('dp', 'seq')), may hold values from -6 to 6
- key_heads: bfloat16 [4096, 512], P(('dp', 'seq')), may hold values from -6 to 6
- value_heads: bfloat16 [4096, 512], P(('dp', 'seq')), may hold values from -6 to 6
- upper_cotangent: bfloat16 [4096, 4096], P(('dp', 'seq')), may hold values from -1.5 to 1.5
- readout: bfloat16 [32, 128], replicated, may hold values from -0.09375 to 0.09375
- base_value: float32 [4096], P(('dp', 'seq')), may hold values from -4 to 4
- old_values: float32 [4096], P(('dp', 'seq')), may hold values from -5 to 5
- returns: float32 [4096], P(('dp', 'seq')), may hold values from -6 to 6
- source_index: int32 [8, 512], P('dp'), may hold values from 0 to 511, as said below
- doc_lengths: int32 [8, 4], P('dp'), may hold values from 1 to 256, 512 in all within a row
Outputs:
- values: float32 [4096], P(('dp', 'seq'))
- grad_queries: bfloat16 [4096, 4096], P(('dp', 'seq'))
- grad_key_heads: bfloat16 [4096, 512], P(('dp', 'seq'))
- grad_value_heads: bfloat16 [4096, 512], P(('dp', 'seq'))
- grad_readout: float32 [32, 128], P('seq', 'dp')
The draws below stay inside these ranges and needn't reach their ends.
Inputs may be any that keep to these rules, and one draw needn't show every extreme that they name: `source_index`: each row is a permutation of its positions. Of the 128 trainer positions of one seq index, at most 64 take their generator position from the 128 positions of any one seq index, and in every row each seq index reaches 64 with one source; every seq index receives and sends the same multiset of such counts.
All inputs are finite; a program needn't handle non-finite values.
Results may differ from the reference program's by a relative error of at most 0.012.
The reference program's roundings to bfloat16 on the way count: a program that leaves them out, or rounds other values in their place, can miss the bound.
Values may be sent and summed in bfloat16 or wider, within the bound.
No kernel may reach another device: no remote copies, remote signals or barrier semaphores. Data moves between devices by JAX's collectives and lax.ppermute only.
A program may use at most 64 MiB of HBM per device.

```python
import math
import jax
import jax.numpy as jnp
import numpy as np
from jax import lax

H = 32
KVH = 4
HD = 128
T_DEV = 128
DA = 4096
KVD = 512
L = 512
TOKENS = 4096
DOCS = 4
MAXDOC = 256
N_DP = 8
N_SEQ = 4


def source_table(key):
    length = T_DEV * N_SEQ
    capacity = 2 * T_DEV // N_SEQ

    def one_row(row_key):
        split_keys = jax.random.split(row_key, 5)
        chosen = jax.random.permutation(split_keys[0], (N_SEQ - 1) * capacity)[:T_DEV - capacity]
        others = jnp.sum(chosen[:, None] // capacity == jnp.arange(N_SEQ - 1, dtype=jnp.int32)[None, :], axis=0).astype(jnp.int32)
        amounts = jnp.concatenate([jnp.full((1,), capacity, jnp.int32), others])
        row_order = jax.random.permutation(split_keys[1], N_SEQ)
        column_order = jax.random.permutation(split_keys[2], N_SEQ)
        counts = amounts[(row_order[:, None] + column_order[None, :]) % N_SEQ]
        labels = jax.vmap(lambda amount: jnp.repeat(jnp.arange(N_SEQ, dtype=jnp.int32), amount, total_repeat_length=T_DEV))(counts)
        labels = jax.vmap(jax.random.permutation)(jax.random.split(split_keys[3], N_SEQ), labels).reshape(length)
        one_hot = (labels[:, None] == jnp.arange(N_SEQ, dtype=jnp.int32)[None, :]).astype(jnp.int32)
        ranking = jnp.sum((jnp.cumsum(one_hot, axis=0) - 1) * one_hot, axis=1)
        shuffles = jax.vmap(lambda sub_key: jax.random.permutation(sub_key, T_DEV))(jax.random.split(split_keys[4], N_SEQ))
        within = shuffles[labels, ranking]
        return (labels * T_DEV + within).astype(jnp.int32)
    row_keys = jax.vmap(lambda row_number: jax.random.fold_in(jax.random.fold_in(key, 71), row_number))(jnp.arange(N_DP, dtype=jnp.int32))
    return jax.vmap(one_row)(row_keys)


def draw_source_index(key, part):
    return source_table(key)


def base_draw(key):
    own_key = jax.random.fold_in(key, 23)
    return jnp.clip(jax.random.normal(own_key, (TOKENS,), jnp.float32), -4.0, 4.0)


def draw_base_value(key, part):
    return base_draw(key)


def draw_old_values(key, part):
    length = T_DEV * N_SEQ
    noise = jnp.clip(jax.random.normal(jax.random.fold_in(key, 29), (TOKENS,), jnp.float32), -4.0, 4.0)
    trainer = base_draw(key) + 0.25 * noise
    sources = source_table(key)
    offsets = (jnp.arange(N_DP, dtype=jnp.int32) * length)[:, None]
    flat_index = (sources + offsets).reshape(TOKENS)
    return jnp.zeros((TOKENS,), jnp.float32).at[flat_index].set(trainer)


def draw_queries(key, part):
    own_key = jax.random.fold_in(key, 61)
    drawn = jnp.clip(jax.random.normal(own_key, (TOKENS, H, HD), jnp.float32), -6.0, 6.0)
    return drawn.reshape(TOKENS, H * HD).astype(jnp.bfloat16)


def draw_key_heads(key, part):
    own_key = jax.random.fold_in(key, 67)
    drawn = jnp.clip(jax.random.normal(own_key, (TOKENS, KVH, HD), jnp.float32), -6.0, 6.0)
    return drawn.reshape(TOKENS, KVH * HD).astype(jnp.bfloat16)


def block_levels(rng, dims, cuts, low, top_value):
    def one(axis_at, parts):
        heights = jax.random.uniform(jax.random.fold_in(jax.random.fold_in(rng, 6), axis_at), (parts,), jnp.float32, low / len(cuts), top_value / len(cuts))
        return jnp.repeat(jnp.exp(heights), dims[axis_at] // parts).reshape((-1,) + (1,) * (len(dims) - axis_at - 1))

    level = one(*cuts[0])
    for cut in cuts[1:]:
        level = level * one(*cut)
    return level


def length_profile(count, total, bound, lean):
    portions = [(1 << 20) // math.isqrt(standing ** lean) + 1 for standing in range(2, count + 1)]
    spare, holding = total - bound - (count - 1), [1] * (count - 1)
    while spare > 0:
        movable = [i for i in range(count - 1) if holding[i] < bound]
        mass, remaining = sum([portions[i] for i in movable]), spare
        for i in movable:
            extra = min(bound - holding[i], max(1, remaining * portions[i] // mass), spare)
            holding[i] = holding[i] + extra
            spare = spare - extra
    return np.array([bound] + holding)


def uneven(rng, count, total, bound, slope):
    if count == 2:
        one = jax.random.randint(rng, (), max(1, total - bound), min(bound, total - 1) + 1)
        return jnp.stack([one, total - one])
    tallies = jnp.asarray(length_profile(count, total, bound, slope), jnp.int32)
    pairs = (count - 1) // 2
    source_of, taker = tallies[1:1 + 2 * pairs:2], tallies[2:2 + 2 * pairs:2]
    room = jnp.minimum(source_of - 1, bound - taker)
    passed = jax.random.randint(jax.random.fold_in(rng, 1), (pairs,), 0, 1 << 20) % (room + 1)
    tallies = tallies.at[1:1 + 2 * pairs:2].set(source_of - passed).at[2:2 + 2 * pairs:2].set(taker + passed)
    return tallies[jax.random.permutation(jax.random.fold_in(rng, 2), count)]


def scatter_about(key, dims, width, reach, shards=(), held_as=jnp.bfloat16):
    values = jax.random.normal(key, dims, jnp.float32) * width
    if len(shards) > 0:
        values = block_levels(key, dims, shards, -0.22, 0.18) * values
    return jnp.clip(values, min=-reach, max=reach).astype(held_as)


def setup_inputs(seed: int = 0) -> dict:
    seeds = jax.random.split(jax.random.key(seed), 11)
    queries = draw_queries(jax.random.fold_in(seeds[10], 71), 0)
    key_heads = draw_key_heads(jax.random.fold_in(seeds[10], 71), 0)
    value_heads = scatter_about(seeds[2], (TOKENS, KVD), 1.0, 6.0, ((0, 32),))
    upper_cotangent = scatter_about(seeds[3], (TOKENS, DA), 0.25, 1.5, ((0, 32),))
    readout = scatter_about(seeds[4], (H, HD), (H * HD) ** -0.5, 0.09375)
    base_value = draw_base_value(jax.random.fold_in(seeds[10], 71), 0)
    old_values = draw_old_values(jax.random.fold_in(seeds[10], 71), 0)
    returns = scatter_about(seeds[7], (TOKENS,), 1.0, 6.0, ((0, 32),), jnp.float32)
    source_index = draw_source_index(jax.random.fold_in(seeds[10], 71), 0)
    doc_lengths = jax.vmap(lambda own: uneven(own, DOCS, L, MAXDOC, 2))(jax.random.split(seeds[9], N_DP)).reshape((N_DP, DOCS)).astype(jnp.int32)
    return dict(queries=queries, key_heads=key_heads, value_heads=value_heads, upper_cotangent=upper_cotangent, readout=readout, base_value=base_value, old_values=old_values, returns=returns, source_index=source_index, doc_lengths=doc_lengths)


clip_range = 0.2
smooth_width = 0.1
loss_scale = 16.0

def doc_starts(doc_sizes, length):
    doc_ends = jnp.cumsum(doc_sizes).astype(jnp.int32)
    doc_firsts = (doc_ends - doc_sizes).astype(jnp.int32)
    positions = jnp.arange(length, dtype=jnp.int32)
    inside = (positions[:, None] >= doc_firsts[None, :]) & (positions[:, None] < doc_ends[None, :])
    return lax.optimization_barrier(jnp.sum(jnp.where(inside, doc_firsts[None, :], 0), axis=1)).astype(jnp.int32)

def value_grad(values, old_now, return_now):
    ratio = jnp.tanh((values - old_now) / clip_range)
    clipped = old_now + clip_range * ratio
    plain_gap = values - return_now
    clip_gap = clipped - return_now
    mixing = jax.nn.sigmoid((plain_gap * plain_gap - clip_gap * clip_gap) / smooth_width)
    return loss_scale * (mixing * plain_gap + (1.0 - mixing) * clip_gap * (1.0 - ratio * ratio))

def rounded(array):
    return lax.optimization_barrier(array.astype(jnp.bfloat16)).astype(jnp.float32)

def reference(queries, key_heads, value_heads, upper_cotangent, readout, base_value, old_values, returns, source_index, doc_lengths):
    length = T_DEV * N_SEQ
    group = H // KVH
    share_heads = min(group, H // N_SEQ)
    score_scale = HD ** (-0.5)
    read_grid = readout.astype(jnp.float32).reshape(KVH, group, HD)

    def block_sum(each):
        partial_sums = rounded(lax.optimization_barrier(jnp.sum(each.reshape(group // share_heads, share_heads, length, HD), axis=1)))
        return lax.optimization_barrier(jnp.sum(partial_sums, axis=0)).astype(jnp.bfloat16)

    def per_row(row_args):
        query_row, key_row, value_row, upper_row, base_row, old_row, return_row, source_row, size_row = row_args
        starts = doc_starts(size_row, length)
        positions = jnp.arange(length, dtype=jnp.int32)
        visible = (starts[:, None] == starts[None, :]) & (positions[None, :] <= positions[:, None])

        def forward_group(group_args):
            query_group, key_one, value_one = group_args
            scores = jnp.einsum('qah,kh->aqk', query_group.astype(jnp.float32), key_one.astype(jnp.float32)) * score_scale
            masked = jnp.where(visible[None], scores, -1e+30)
            row_max = lax.optimization_barrier(jnp.max(masked, axis=2, keepdims=True))
            row_total = lax.optimization_barrier(jnp.sum(jnp.where(visible[None], jnp.exp(masked - row_max), 0.0), axis=2, keepdims=True))
            log_total = row_max + jnp.log(row_total)
            weights = rounded(jnp.where(visible[None], jnp.exp(masked - log_total), 0.0))
            attn_out = jnp.einsum('aqk,kh->qah', weights, value_one.astype(jnp.float32)).astype(jnp.bfloat16)
            return (attn_out, log_total[:, :, 0])
        attn_out, log_total = lax.map(forward_group, (query_row.transpose(1, 0, 2, 3), key_row.transpose(1, 0, 2), value_row.transpose(1, 0, 2)))
        attn_out = attn_out.transpose(1, 0, 2, 3)
        out_float = attn_out.astype(jnp.float32)
        values = base_row + jnp.einsum('qcah,cah->q', out_float, read_grid)
        old_now = jnp.take(old_row, source_row)
        return_now = jnp.take(return_row, source_row)
        value_cot = value_grad(values, old_now, return_now)
        out_cot = (upper_row.astype(jnp.float32) + value_cot[:, None, None, None] * read_grid[None]).astype(jnp.bfloat16)
        deltas = lax.optimization_barrier(jnp.sum(out_cot.astype(jnp.float32) * out_float, axis=3))
        readout_part = jnp.einsum('q,qcah->cah', value_cot, out_float)

        def backward_group(group_args):
            query_group, key_one, value_one, cot_group, log_group, delta_group = group_args
            query_float = query_group.astype(jnp.float32)
            key_float = key_one.astype(jnp.float32)
            cot_float = cot_group.astype(jnp.float32)
            scores = jnp.einsum('qah,kh->aqk', query_float, key_float) * score_scale
            masked = jnp.where(visible[None], scores, -1e+30)
            weights = jnp.where(visible[None], jnp.exp(masked - log_group[:, :, None]), 0.0)
            grad_weights = jnp.einsum('qah,kh->aqk', cot_float, value_one.astype(jnp.float32))
            grad_scores = rounded(weights * (grad_weights - delta_group.T[:, :, None]) * score_scale)
            grad_query = jnp.einsum('aqk,kh->qah', grad_scores, key_float).astype(jnp.bfloat16)
            key_each = jnp.einsum('aqk,qah->akh', grad_scores, query_float)
            value_each = jnp.einsum('aqk,qah->akh', rounded(weights), cot_float)
            return (grad_query, block_sum(key_each), block_sum(value_each))
        grad_query, grad_key, grad_value = lax.map(backward_group, (query_row.transpose(1, 0, 2, 3), key_row.transpose(1, 0, 2), value_row.transpose(1, 0, 2), out_cot.transpose(1, 0, 2, 3), log_total, deltas.transpose(1, 0, 2)))
        grad_query = grad_query.transpose(1, 0, 2, 3).reshape(length, H * HD)
        grad_key = grad_key.transpose(1, 0, 2).reshape(length, KVH * HD)
        grad_value = grad_value.transpose(1, 0, 2).reshape(length, KVH * HD)
        return (values, grad_query, grad_key, grad_value, readout_part)
    row_inputs = (queries.reshape(N_DP, length, KVH, group, HD), key_heads.reshape(N_DP, length, KVH, HD), value_heads.reshape(N_DP, length, KVH, HD), upper_cotangent.reshape(N_DP, length, KVH, group, HD), base_value.reshape(N_DP, length), old_values.reshape(N_DP, length), returns.reshape(N_DP, length), source_index, doc_lengths)
    values, grad_queries, grad_keys, grad_values, readout_parts = lax.map(per_row, row_inputs)
    return (values.reshape(N_DP * length), grad_queries.reshape(N_DP * length, H * HD), grad_keys.reshape(N_DP * length, KVH * HD), grad_values.reshape(N_DP * length, KVH * HD), lax.optimization_barrier(jnp.sum(readout_parts, axis=0)).reshape(H, HD))
```

```python
import functools

import jax
import jax.numpy as jnp
from jax import lax
from jax.experimental import pallas as pl
from jax.experimental.pallas import tpu as pltpu
from jax.sharding import PartitionSpec as P

clip_range = 0.2
smooth_width = 0.1
loss_scale = 16.0
log2e = 1.4426950408889634


def value_grad(values, old_now, return_now):
    ratio = jnp.tanh((values - old_now) / clip_range)
    clipped = old_now + clip_range * ratio
    plain_gap = values - return_now
    clip_gap = clipped - return_now
    mixing = jax.nn.sigmoid((plain_gap * plain_gap - clip_gap * clip_gap) / smooth_width)
    return loss_scale * (mixing * plain_gap + (1.0 - mixing) * clip_gap * (1.0 - ratio * ratio))


def dot(left, right, left_dim, right_dim):
    return lax.dot_general(
        left,
        right,
        (((left_dim,), (right_dim,)), ((), ())),
        preferred_element_type=jnp.float32,
    )


def attend_kernel(
    seq_count,
    back,
    kv_count,
    doc_ref,
    source_ref,
    base_ref,
    readout_ref,
    query_ref,
    upper_ref,
    *refs,
):
    pair_refs = refs[:seq_count]
    key_refs = refs[seq_count : seq_count + back + 1]
    value_refs = refs[seq_count + back + 1 : seq_count + 2 * back + 2]
    refs = refs[seq_count + 2 * back + 2 :]
    values_ref, grad_query_ref, readout_part_ref = refs[:3]
    grad_pair_refs = refs[3 : back + 3]
    own_key_ref, own_value_ref = refs[back + 3 : back + 5]
    weight_ref, out_ref = refs[back + 5 :]

    tok_dev = query_ref.shape[0]
    head_count, head_size = readout_ref.shape
    per_group = head_count // kv_count
    span = (back + 1) * tok_dev
    rank = lax.axis_index("seq")
    scale = head_size**-0.5

    rows = lax.broadcasted_iota(jnp.int32, (tok_dev, span), 0) + rank * tok_dev
    cols = lax.broadcasted_iota(jnp.int32, (tok_dev, span), 1) + (rank - back) * tok_dev
    first = jnp.zeros((tok_dev, span), jnp.int32)
    start = 0
    for doc in range(doc_ref.shape[1] - 1):
        size = doc_ref[0, doc]
        start = start + size
        first = first + jnp.where(rows >= start, size, 0)
    bias = jnp.where((cols <= rows) & (cols >= first), 0.0, -1e30).astype(jnp.float32)

    def group_keys(source_refs, group):
        lanes = slice(group * head_size, (group + 1) * head_size)
        return jnp.concatenate([ref[:, lanes] for ref in reversed(source_refs)], axis=0)

    def stacked(ref, group):
        heads = range(group * per_group, (group + 1) * per_group)
        return jnp.concatenate(
            [ref[:, h * head_size : (h + 1) * head_size] for h in heads], axis=0
        )

    total = jnp.zeros((tok_dev, head_size), jnp.float32)
    for group in range(kv_count):
        scores = dot(stacked(query_ref, group), group_keys(key_refs, group), 1, 1)
        masked = scores.reshape(per_group, tok_dev, span) * (scale * log2e) + bias[None]
        top = jnp.max(masked, axis=2, keepdims=True)
        raised = jnp.exp2(masked - top)
        weights = raised * (1.0 / jnp.sum(raised, axis=2, keepdims=True))
        weights = weights.reshape(per_group * tok_dev, span)
        weight_ref[group] = weights
        out = dot(weights.astype(jnp.bfloat16), group_keys(value_refs, group), 1, 0)
        out = out.astype(jnp.bfloat16)
        out_ref[group] = out
        for at in range(per_group):
            h = group * per_group + at
            total = total + out[at * tok_dev : (at + 1) * tok_dev].astype(
                jnp.float32
            ) * readout_ref[h : h + 1, :].astype(jnp.float32)

    square = (tok_dev, tok_dev)
    diagonal = lax.broadcasted_iota(jnp.int32, square, 0) == lax.broadcasted_iota(
        jnp.int32, square, 1
    )

    def as_column(row):
        return jnp.sum(jnp.where(diagonal, row, jnp.zeros_like(row)), axis=1, keepdims=True)

    own_sources = as_column(
        source_ref[:, pl.ds(pl.multiple_of(rank * tok_dev, tok_dev), tok_dev)].astype(jnp.float32)
    )
    lanes = lax.broadcasted_iota(jnp.int32, square, 1)
    old_now = jnp.zeros((tok_dev, 1), jnp.float32)
    return_now = jnp.zeros((tok_dev, 1), jnp.float32)
    for shift in range(seq_count):
        owner = lax.rem(rank - shift + seq_count, seq_count)
        chosen = (lanes + owner * tok_dev).astype(jnp.float32) == own_sources
        pair = pair_refs[shift]
        old_now = old_now + jnp.sum(jnp.where(chosen, pair[0:1, :], 0.0), axis=1, keepdims=True)
        return_now = return_now + jnp.sum(
            jnp.where(chosen, pair[1:2, :], 0.0), axis=1, keepdims=True
        )
    values = as_column(base_ref[...]) + jnp.sum(total, axis=1, keepdims=True)
    value_cot = value_grad(values, old_now, return_now)
    values_ref[...] = jnp.sum(jnp.where(diagonal, values, 0.0), axis=0, keepdims=True)

    for group in range(kv_count):
        cots, deltas = [], []
        for at in range(per_group):
            h = group * per_group + at
            lanes_h = slice(h * head_size, (h + 1) * head_size)
            out = out_ref[group, at * tok_dev : (at + 1) * tok_dev, :].astype(jnp.float32)
            readout_part_ref[h : h + 1, :] = jnp.sum(value_cot * out, axis=0, keepdims=True)
            cot = (
                upper_ref[:, lanes_h].astype(jnp.float32)
                + value_cot * readout_ref[h : h + 1, :].astype(jnp.float32)
            ).astype(jnp.bfloat16)
            cots.append(cot)
            deltas.append(jnp.sum(cot.astype(jnp.float32) * out, axis=1, keepdims=True))
        cot = jnp.concatenate(cots, axis=0)
        delta = jnp.concatenate(deltas, axis=0)
        weights = weight_ref[group]
        keys = group_keys(key_refs, group)
        grad_weights = dot(cot, group_keys(value_refs, group), 1, 1)
        grad_scores = (weights * (grad_weights - delta) * scale).astype(jnp.bfloat16)
        grad_query = dot(grad_scores, keys, 1, 0).astype(jnp.bfloat16)
        for at in range(per_group):
            h = group * per_group + at
            grad_query_ref[:, h * head_size : (h + 1) * head_size] = grad_query[
                at * tok_dev : (at + 1) * tok_dev
            ]
        grad_key = dot(grad_scores, stacked(query_ref, group), 0, 0)
        grad_value = dot(weights.astype(jnp.bfloat16), cot, 0, 0)
        lanes_c = slice(group * head_size, (group + 1) * head_size)
        lanes_v = slice((kv_count + group) * head_size, (kv_count + group + 1) * head_size)
        own = slice(back * tok_dev, (back + 1) * tok_dev)
        own_key_ref[:, lanes_c] = grad_key[own]
        own_value_ref[:, lanes_c] = grad_value[own]
        for step in range(1, back + 1):
            block = slice((back - step) * tok_dev, (back - step + 1) * tok_dev)
            grad_pair_refs[step - 1][:, lanes_c] = grad_key[block].astype(jnp.bfloat16)
            grad_pair_refs[step - 1][:, lanes_v] = grad_value[block].astype(jnp.bfloat16)


def combine_kernel(back, own_key_ref, own_value_ref, *refs):
    pair_refs, (grad_key_ref, grad_value_ref) = refs[:back], refs[back:]
    width = own_key_ref.shape[1]
    for part, own_ref, out_ref in (
        (0, own_key_ref, grad_key_ref),
        (1, own_value_ref, grad_value_ref),
    ):
        total = own_ref[...]
        for pair in pair_refs:
            total = total + pair[:, part * width : (part + 1) * width].astype(jnp.float32)
        out_ref[...] = total.astype(jnp.bfloat16)


def on_device(
    queries,
    key_heads,
    value_heads,
    upper_cotangent,
    readout,
    base_value,
    old_values,
    returns,
    source_index,
    doc_lengths,
):
    seq_count = lax.axis_size("seq")
    dp_count = lax.axis_size("dp")
    tok_dev, model_width = queries.shape
    head_count, head_size = readout.shape
    kv_width = key_heads.shape[1]
    kv_count = kv_width // head_size
    per_group = head_count // kv_count
    longest = tok_dev * seq_count // 2
    back = min(seq_count - 1, (longest - 1 + tok_dev - 1) // tok_dev)
    span = (back + 1) * tok_dev

    def rotate(array, shift):
        pairs = [(i, (i + shift) % seq_count) for i in range(seq_count)]
        return lax.ppermute(array, "seq", pairs)

    keys = [key_heads] + [rotate(key_heads, step) for step in range(1, back + 1)]
    values_in = [value_heads] + [rotate(value_heads, step) for step in range(1, back + 1)]
    pair = jnp.stack([old_values, returns])
    pairs = [pair] + [rotate(pair, shift) for shift in range(1, seq_count)]

    vmem = pl.BlockSpec(memory_space=pltpu.VMEM)
    smem = pl.BlockSpec(memory_space=pltpu.SMEM)
    outs = pl.pallas_call(
        functools.partial(attend_kernel, seq_count, back, kv_count),
        in_specs=[smem] + [vmem] * (5 + seq_count + 2 * (back + 1)),
        out_specs=[vmem] * (5 + back),
        out_shape=[
            jax.ShapeDtypeStruct((1, tok_dev), jnp.float32),
            jax.ShapeDtypeStruct((tok_dev, model_width), jnp.bfloat16),
            jax.ShapeDtypeStruct((head_count, head_size), jnp.float32),
        ]
        + [jax.ShapeDtypeStruct((tok_dev, 2 * kv_width), jnp.bfloat16)] * back
        + [jax.ShapeDtypeStruct((tok_dev, kv_width), jnp.float32)] * 2,
        scratch_shapes=[
            pltpu.VMEM((kv_count, per_group * tok_dev, span), jnp.float32),
            pltpu.VMEM((kv_count, per_group * tok_dev, head_size), jnp.bfloat16),
        ],
        compiler_params=pltpu.CompilerParams(vmem_limit_bytes=60 * 1024 * 1024),
        name="attend",
    )(
        doc_lengths,
        source_index,
        base_value.reshape(1, tok_dev),
        readout,
        queries,
        upper_cotangent,
        *pairs,
        *keys,
        *values_in,
    )
    values, grad_queries, readout_part = outs[:3]
    grad_pairs, (own_key, own_value) = outs[3 : 3 + back], outs[3 + back :]
    returned = [rotate(grad_pairs[step - 1], -step) for step in range(1, back + 1)]

    own_heads, own_size = head_count // seq_count, head_size // dp_count
    parts = readout_part.reshape(seq_count, own_heads, dp_count, own_size)
    parts = parts.transpose(2, 0, 1, 3).reshape(dp_count * seq_count, 1, own_heads * own_size)
    parts = lax.all_to_all(parts, ("dp", "seq"), 0, 0, tiled=True)
    grad_readout = jnp.sum(parts, axis=0).reshape(own_heads, own_size)

    grad_key_heads, grad_value_heads = pl.pallas_call(
        functools.partial(combine_kernel, back),
        in_specs=[vmem] * (2 + back),
        out_specs=[vmem] * 2,
        out_shape=[jax.ShapeDtypeStruct((tok_dev, kv_width), jnp.bfloat16)] * 2,
        name="combine",
    )(own_key, own_value, *returned)
    return (values.reshape(tok_dev), grad_queries, grad_key_heads, grad_value_heads, grad_readout)


def solution(mesh):
    return jax.shard_map(
        on_device,
        mesh=mesh,
        in_specs=(
            P(("dp", "seq"), None),
            P(("dp", "seq"), None),
            P(("dp", "seq"), None),
            P(("dp", "seq"), None),
            P(),
            P(("dp", "seq")),
            P(("dp", "seq")),
            P(("dp", "seq")),
            P("dp", None),
            P("dp", None),
        ),
        out_specs=(
            P(("dp", "seq")),
            P(("dp", "seq"), None),
            P(("dp", "seq"), None),
            P(("dp", "seq"), None),
            P("seq", "dp"),
        ),
        check_vma=False,
    )
```

```python
import functools

import jax
import jax.numpy as jnp
from jax import lax
from jax.experimental import pallas as pl
from jax.experimental.pallas import tpu as pltpu
from jax.sharding import PartitionSpec as P


clip_range = 0.2
smooth_width = 0.1
loss_scale = 16.0
log2e = 1.4426950408889634


def value_grad(values, old_now, return_now):
    ratio = jnp.tanh((values - old_now) / clip_range)
    clipped = old_now + clip_range * ratio
    plain_gap = values - return_now
    clip_gap = clipped - return_now
    mixing = jax.nn.sigmoid((plain_gap * plain_gap - clip_gap * clip_gap) / smooth_width)
    return loss_scale * (mixing * plain_gap + (1.0 - mixing) * clip_gap * (1.0 - ratio * ratio))


def dot(left, right, left_dim, right_dim):
    return lax.dot_general(
        left,
        right,
        (((left_dim,), (right_dim,)), ((), ())),
        preferred_element_type=jnp.float32,
    )


def block_bias(doc_ref, rank, tok_dev, key_block, blocks):
    shape = (blocks * tok_dev, tok_dev)
    keys = lax.broadcasted_iota(jnp.int32, shape, 0) + key_block * tok_dev
    places = lax.broadcasted_iota(jnp.int32, shape, 1) + rank * tok_dev
    first = jnp.zeros(shape, jnp.int32)
    start = 0
    for doc in range(doc_ref.shape[1] - 1):
        size = doc_ref[0, doc]
        start = start + size
        first = first + jnp.where(places >= start, size, 0)
    return jnp.where((keys <= places) & (keys >= first), 0.0, -1e30).astype(jnp.float32)


def diagonal_of(size):
    shape = (size, size)
    return lax.broadcasted_iota(jnp.int32, shape, 0) == lax.broadcasted_iota(jnp.int32, shape, 1)


def as_column(row, diagonal):
    return jnp.sum(jnp.where(diagonal, row, jnp.zeros_like(row)), axis=1, keepdims=True)


def lanes_of(group, size):
    return slice(group * size, (group + 1) * size)


def group_rows(refs, group, size):
    return jnp.concatenate([ref[:, lanes_of(group, size)] for ref in reversed(refs)], axis=0)


def stacked(ref, group, per_group, size):
    heads = range(group * per_group, (group + 1) * per_group)
    return jnp.concatenate([ref[:, lanes_of(h, size)] for h in heads], axis=0)


def own_kernel(kv_count, doc_ref, query_ref, key_ref, value_ref, qt_ref, raised_ref, sum_ref, stat_ref):
    tok_dev, head_size = query_ref.shape[0], key_ref.shape[1] // kv_count
    per_group = query_ref.shape[1] // head_size // kv_count
    rank = lax.axis_index("seq")
    factor = head_size**-0.5 * log2e
    bias = jnp.tile(block_bias(doc_ref, rank, tok_dev, rank, 1), (1, per_group))
    for group in range(kv_count):
        for at in range(per_group):
            tile = query_ref[:, lanes_of(group * per_group + at, head_size)]
            qt_ref[group, :, lanes_of(at, tok_dev)] = tile.T
        scores = dot(key_ref[:, lanes_of(group, head_size)], qt_ref[group], 1, 0)
        scores = scores * factor + bias
        top = jnp.max(scores, axis=0, keepdims=True)
        raised = jnp.exp2(scores - top)
        raised_ref[group] = raised
        stat_ref[0, group : group + 1, :] = top
        stat_ref[1, group : group + 1, :] = jnp.sum(raised, axis=0, keepdims=True)
        sum_ref[group] = dot(
            value_ref[:, lanes_of(group, head_size)], raised.astype(jnp.bfloat16), 0, 0
        )


def source_kernel(seq_count, source_ref, *refs):
    pair_refs, out_ref = refs[:seq_count], refs[seq_count]
    tok_dev = out_ref.shape[1]
    rank = lax.axis_index("seq")
    diagonal = diagonal_of(tok_dev)
    places = lax.broadcasted_iota(jnp.int32, (tok_dev, tok_dev), 0)
    own = source_ref[:, pl.ds(pl.multiple_of(rank * tok_dev, tok_dev), tok_dev)]
    old_now = jnp.zeros((1, tok_dev), jnp.float32)
    return_now = jnp.zeros((1, tok_dev), jnp.float32)
    for shift in range(seq_count):
        owner = lax.rem(rank - shift + seq_count, seq_count)
        chosen = places + owner * tok_dev == own
        pair = pair_refs[shift]
        old_now = old_now + jnp.sum(
            jnp.where(chosen, as_column(pair[0:1, :], diagonal), 0.0), axis=0, keepdims=True
        )
        return_now = return_now + jnp.sum(
            jnp.where(chosen, as_column(pair[1:2, :], diagonal), 0.0), axis=0, keepdims=True
        )
    out_ref[0:1, :] = old_now
    out_ref[1:2, :] = return_now


def forward_kernel(
    back, kv_count, doc_ref, now_ref, base_ref, readout_ref, qt_ref, sum_ref, stat_ref, upper_ref, *refs
):
    key_refs, value_refs = refs[:back], refs[back : 2 * back]
    values_ref, cot_row_ref, raised_ref, out_ref, cot_ref, norm_ref = refs[2 * back : 2 * back + 6]
    grad_value_refs = refs[2 * back + 6 :]
    tok_dev = upper_ref.shape[0]
    head_count, head_size = readout_ref.shape
    per_group = head_count // kv_count
    rank = lax.axis_index("seq")
    factor = head_size**-0.5 * log2e
    bias = jnp.tile(block_bias(doc_ref, rank, tok_dev, rank - back, back), (1, per_group))
    total = base_ref[...]
    scales = []
    for group in range(kv_count):
        scores = dot(group_rows(key_refs, group, head_size), qt_ref[group], 1, 0)
        scores = scores * factor + bias
        own_top = stat_ref[0, group : group + 1, :]
        top = jnp.maximum(jnp.max(scores, axis=0, keepdims=True), own_top)
        raised = jnp.exp2(scores - top)
        raised_ref[group] = raised
        shrink = jnp.exp2(own_top - top)
        inverse = 1.0 / (
            jnp.sum(raised, axis=0, keepdims=True) + shrink * stat_ref[1, group : group + 1, :]
        )
        norm_ref[0, group : group + 1, :] = inverse
        norm_ref[1, group : group + 1, :] = shrink * inverse
        scales.append(inverse)
        out = dot(group_rows(value_refs, group, head_size), raised.astype(jnp.bfloat16), 0, 0)
        out = ((out + sum_ref[group] * shrink) * inverse).astype(jnp.bfloat16)
        out_ref[group] = out
        terms = dot(readout_ref[group * per_group : (group + 1) * per_group, :], out, 1, 0)
        for at in range(per_group):
            total = total + terms[at : at + 1, lanes_of(at, tok_dev)]
    values_ref[...] = total
    value_cot = value_grad(total, now_ref[0:1, :], now_ref[1:2, :])
    cot_row_ref[...] = value_cot
    column = jnp.broadcast_to(as_column(value_cot, diagonal_of(tok_dev)), (tok_dev, head_size))
    for group in range(kv_count):
        cots = []
        for at in range(per_group):
            h = group * per_group + at
            cots.append(
                (
                    upper_ref[:, lanes_of(h, head_size)].astype(jnp.float32)
                    + column * readout_ref[h : h + 1, :].astype(jnp.float32)
                ).astype(jnp.bfloat16)
            )
        cot = jnp.concatenate(cots, axis=0)
        cot_ref[group] = cot
        weights = (raised_ref[group] * scales[group]).astype(jnp.bfloat16)
        grad_value = dot(weights, cot, 1, 0).astype(jnp.bfloat16)
        for step in range(1, back + 1):
            grad_value_refs[step - 1][:, lanes_of(group, head_size)] = grad_value[
                (back - step) * tok_dev : (back - step + 1) * tok_dev
            ]


def key_grad_kernel(back, kv_count, raised_ref, norm_ref, cot_ref, out_ref, query_ref, *refs):
    value_refs = refs[:back]
    delta_ref, ct_ref, grad_score_ref = refs[back : back + 3]
    grad_key_refs = refs[back + 3 :]
    tok_dev = query_ref.shape[0]
    head_size = out_ref.shape[1]
    per_group = query_ref.shape[1] // head_size // kv_count
    scale = head_size**-0.5
    for group in range(kv_count):
        for at in range(per_group):
            ct_ref[group, :, lanes_of(at, tok_dev)] = cot_ref[
                group, at * tok_dev : (at + 1) * tok_dev, :
            ].T
        turned = ct_ref[group]
        delta = jnp.sum(
            turned.astype(jnp.float32) * out_ref[group].astype(jnp.float32), axis=0, keepdims=True
        )
        delta_ref[group : group + 1, :] = delta
        grad_weights = dot(group_rows(value_refs, group, head_size), turned, 1, 0)
        grad_scores = raised_ref[group] * (
            (grad_weights - delta) * (norm_ref[0, group : group + 1, :] * scale)
        )
        grad_scores = grad_scores.astype(jnp.bfloat16)
        grad_score_ref[group] = grad_scores
        grad_key = dot(grad_scores, stacked(query_ref, group, per_group, head_size), 1, 0)
        grad_key = grad_key.astype(jnp.bfloat16)
        for step in range(1, back + 1):
            grad_key_refs[step - 1][:, lanes_of(group, head_size)] = grad_key[
                (back - step) * tok_dev : (back - step + 1) * tok_dev
            ]


def readout_kernel(seq_count, kv_count, cot_row_ref, out_ref, *refs):
    part_refs, whole_ref = refs[:seq_count], refs[seq_count]
    tok_dev = cot_row_ref.shape[1]
    per_group = out_ref.shape[2] // tok_dev
    own_heads = part_refs[0].shape[0]
    rank = lax.axis_index("seq")
    row = cot_row_ref[...]
    high = row.astype(jnp.bfloat16).astype(jnp.float32)
    middle = (row - high).astype(jnp.bfloat16).astype(jnp.float32)
    low = row - high - middle
    places = lax.broadcasted_iota(jnp.int32, (16, tok_dev), 0)
    rows = jnp.where(
        places == 0, high, jnp.where(places == 1, middle, jnp.where(places == 2, low, 0.0))
    ).astype(jnp.bfloat16)
    for group in range(kv_count):
        for at in range(per_group):
            h = group * per_group + at
            terms = dot(rows, out_ref[group, :, lanes_of(at, tok_dev)], 1, 1)
            whole_ref[h : h + 1, :] = jnp.sum(terms, axis=0, keepdims=True)
    for shift in range(seq_count):
        owner = lax.rem(rank + shift, seq_count)
        part_refs[shift][...] = whole_ref[
            pl.ds(pl.multiple_of(owner * own_heads, own_heads), own_heads), :
        ]


def query_grad_kernel(
    back, kv_count, raised_ref, norm_ref, delta_ref, cot_ref, ct_ref, score_ref, query_ref, *refs
):
    key_refs, value_ref = refs[: back + 1], refs[back + 1]
    grad_query_ref, own_key_ref, own_value_ref = refs[back + 2 :]
    tok_dev = query_ref.shape[0]
    head_size = ct_ref.shape[1]
    per_group = query_ref.shape[1] // head_size // kv_count
    scale = head_size**-0.5
    for group in range(kv_count):
        lanes = lanes_of(group, head_size)
        weights = raised_ref[group] * norm_ref[1, group : group + 1, :]
        own_value_ref[:, lanes] = dot(weights.astype(jnp.bfloat16), cot_ref[group], 1, 0)
        grad_weights = dot(value_ref[:, lanes], ct_ref[group], 1, 0)
        grad_scores = weights * ((grad_weights - delta_ref[group : group + 1, :]) * scale)
        grad_scores = grad_scores.astype(jnp.bfloat16)
        own_key_ref[:, lanes] = dot(
            grad_scores, stacked(query_ref, group, per_group, head_size), 1, 0
        )
        scores = jnp.concatenate([score_ref[group], grad_scores], axis=0)
        grad_query = dot(group_rows(key_refs, group, head_size), scores, 0, 0)
        for at in range(per_group):
            grad_query_ref[:, lanes_of(group * per_group + at, head_size)] = grad_query[
                :, lanes_of(at, tok_dev)
            ].T.astype(jnp.bfloat16)


def part_sum_kernel(*refs):
    total = refs[0][...]
    for ref in refs[1:-1]:
        total = total + ref[...]
    refs[-1][...] = total


def combine_kernel(back, dp_count, own_key_ref, own_value_ref, *refs):
    key_refs, value_refs, part_refs = refs[:back], refs[back : 2 * back], refs[2 * back : -3]
    grad_key_ref, grad_value_ref, grad_readout_ref = refs[-3:]
    for own_ref, other_refs, out_ref in (
        (own_key_ref, key_refs, grad_key_ref),
        (own_value_ref, value_refs, grad_value_ref),
    ):
        total = own_ref[...]
        for other in other_refs:
            total = total + other[...].astype(jnp.float32)
        out_ref[...] = total.astype(jnp.bfloat16)
    total = part_refs[0][...]
    for part in part_refs[1:]:
        total = total + part[...]
    width, own_size = total.shape[1], grad_readout_ref.shape[1]
    shift = lax.rem(width - lax.axis_index("dp") * own_size, width)
    grad_readout_ref[...] = pltpu.roll(total, shift, 1)[:, :own_size]


def on_device(
    queries,
    key_heads,
    value_heads,
    upper_cotangent,
    readout,
    base_value,
    old_values,
    returns,
    source_index,
    doc_lengths,
):
    seq_count = lax.axis_size("seq")
    dp_count = lax.axis_size("dp")
    tok_dev, model_width = queries.shape
    head_count, head_size = readout.shape
    kv_width = key_heads.shape[1]
    kv_count = kv_width // head_size
    per_group = head_count // kv_count
    wide = per_group * tok_dev
    own_heads, own_size = head_count // seq_count, head_size // dp_count
    longest = tok_dev * seq_count // 2
    back = min(seq_count - 1, (longest - 1 + tok_dev - 1) // tok_dev)
    span = (back + 1) * tok_dev

    def rotate(array, shift, axis="seq"):
        count = lax.axis_size(axis)
        return lax.ppermute(array, axis, [(i, (i + shift) % count) for i in range(count)])

    def call(kernel, name, in_specs, outs, megabytes, flops, scratch=()):
        return pl.pallas_call(
            kernel,
            in_specs=in_specs,
            out_specs=[vmem] * len(outs),
            out_shape=[jax.ShapeDtypeStruct(*out) for out in outs],
            scratch_shapes=list(scratch),
            compiler_params=pltpu.CompilerParams(vmem_limit_bytes=megabytes << 20),
            cost_estimate=pl.CostEstimate(
                flops=flops, bytes_accessed=flops // 1000, transcendentals=0
            ),
            name=name,
        )

    vmem = pl.BlockSpec(memory_space=pltpu.VMEM)
    smem = pl.BlockSpec(memory_space=pltpu.SMEM)
    room = 8 + (kv_count * wide * span * 4 >> 20)
    unit = 2 * head_count * tok_dev * tok_dev * head_size
    f32, bf16 = jnp.float32, jnp.bfloat16
    keys, vals = [], []
    for step in range(1, back + 1):
        keys.append(rotate(key_heads, step))
    for step in range(1, back + 1):
        vals.append(rotate(value_heads, step))
    pair = jnp.stack([old_values, returns])
    pairs = [pair] + [rotate(pair, shift) for shift in range(1, seq_count)]

    turned_query, own_raised, own_sum, own_stat = call(
        functools.partial(own_kernel, kv_count),
        "own_forward",
        [smem] + [vmem] * 3,
        [
            ((kv_count, head_size, wide), bf16),
            ((kv_count, tok_dev, wide), f32),
            ((kv_count, head_size, wide), f32),
            ((2, kv_count, wide), f32),
        ],
        room,
        2 * unit,
    )(doc_lengths, queries, key_heads, value_heads)
    (now,) = call(
        functools.partial(source_kernel, seq_count),
        "source",
        [vmem] * (1 + seq_count),
        [((2, tok_dev), f32)],
        8,
        tok_dev * tok_dev * 4,
    )(source_index, *pairs)
    outs = call(
        functools.partial(forward_kernel, back, kv_count),
        "forward",
        [smem] + [vmem] * (7 + 2 * back),
        [
            ((1, tok_dev), f32),
            ((1, tok_dev), f32),
            ((kv_count, back * tok_dev, wide), f32),
            ((kv_count, head_size, wide), bf16),
            ((kv_count, wide, head_size), bf16),
            ((2, kv_count, wide), f32),
        ]
        + [((tok_dev, kv_width), bf16)] * back,
        room,
        3 * back * unit,
    )(
        doc_lengths,
        now,
        base_value.reshape(1, tok_dev),
        readout,
        turned_query,
        own_sum,
        own_stat,
        upper_cotangent,
        *keys,
        *vals,
    )
    new_values, cot_row, raised, out, cot, norm = outs[:6]
    value_back = [rotate(outs[6 + step - 1], -step) for step in range(1, back + 1)]
    outs = call(
        functools.partial(key_grad_kernel, back, kv_count),
        "key_grad",
        [vmem] * (5 + back),
        [
            ((kv_count, wide), f32),
            ((kv_count, head_size, wide), bf16),
            ((kv_count, back * tok_dev, wide), bf16),
        ]
        + [((tok_dev, kv_width), bf16)] * back,
        room,
        2 * back * unit,
    )(raised, norm, cot, out, queries, *vals)
    delta, turned_cot, grad_scores = outs[:3]
    key_back = [rotate(outs[3 + step - 1], -step) for step in range(1, back + 1)]
    parts = call(
        functools.partial(readout_kernel, seq_count, kv_count),
        "readout_part",
        [vmem] * 2,
        [((own_heads, head_size), f32)] * seq_count,
        8,
        unit // 100,
        [pltpu.VMEM((head_count, head_size), f32)],
    )(cot_row, out)
    parts = [parts[0]] + [rotate(parts[shift], shift) for shift in range(1, seq_count)]
    grad_queries, own_key, own_value = call(
        functools.partial(query_grad_kernel, back, kv_count),
        "query_grad",
        [vmem] * (9 + back),
        [
            ((tok_dev, model_width), bf16),
            ((tok_dev, kv_width), f32),
            ((tok_dev, kv_width), f32),
        ],
        room,
        (4 + back) * unit,
    )(own_raised, norm, delta, cot, turned_cot, grad_scores, queries, key_heads, *keys, value_heads)
    (part,) = call(
        part_sum_kernel, "part_sum", [vmem] * seq_count, [((own_heads, head_size), f32)], 4, 1000
    )(*parts)
    parts = [part] + [rotate(part, shift, "dp") for shift in range(1, dp_count)]
    grad_key_heads, grad_value_heads, grad_readout = call(
        functools.partial(combine_kernel, back, dp_count),
        "combine",
        [vmem] * (2 + 2 * back + dp_count),
        [
            ((tok_dev, kv_width), bf16),
            ((tok_dev, kv_width), bf16),
            ((own_heads, own_size), f32),
        ],
        8,
        unit // 100,
    )(own_key, own_value, *key_back, *value_back, *parts)
    return (
        new_values.reshape(tok_dev),
        grad_queries,
        grad_key_heads,
        grad_value_heads,
        grad_readout,
    )


def solution(mesh):
    return jax.shard_map(
        on_device,
        mesh=mesh,
        in_specs=(
            P(("dp", "seq"), None),
            P(("dp", "seq"), None),
            P(("dp", "seq"), None),
            P(("dp", "seq"), None),
            P(),
            P(("dp", "seq")),
            P(("dp", "seq")),
            P(("dp", "seq")),
            P("dp", None),
            P("dp", None),
        ),
        out_specs=(
            P(("dp", "seq")),
            P(("dp", "seq"), None),
            P(("dp", "seq"), None),
            P(("dp", "seq"), None),
            P("seq", "dp"),
        ),
        check_vma=False,
    )
```

```python
import functools

import jax
import jax.numpy as jnp
from jax import lax
from jax.experimental import pallas as pl
from jax.experimental.pallas import tpu as pltpu
from jax.sharding import PartitionSpec as P


clip_range = 0.2
smooth_width = 0.1
loss_scale = 16.0


def value_grad(values, old_now, return_now):
    ratio = jnp.tanh((values - old_now) / clip_range)
    clipped = old_now + clip_range * ratio
    plain_gap = values - return_now
    clip_gap = clipped - return_now
    mixing = jax.nn.sigmoid((plain_gap * plain_gap - clip_gap * clip_gap) / smooth_width)
    return loss_scale * (mixing * plain_gap + (1.0 - mixing) * clip_gap * (1.0 - ratio * ratio))


def dot(left, right, left_dim, right_dim):
    return lax.dot_general(
        left,
        right,
        (((left_dim,), (right_dim,)), ((), ())),
        preferred_element_type=jnp.float32,
    )


def block_bias(doc_ref, rank, tok_dev, key_block, blocks):
    shape = (blocks * tok_dev, tok_dev)
    keys = lax.broadcasted_iota(jnp.int32, shape, 0) + key_block * tok_dev
    places = lax.broadcasted_iota(jnp.int32, shape, 1) + rank * tok_dev
    first = jnp.zeros(shape, jnp.int32)
    start = 0
    for doc in range(doc_ref.shape[1] - 1):
        size = doc_ref[0, doc]
        start = start + size
        first = first + jnp.where(places >= start, size, 0)
    return jnp.where((keys <= places) & (keys >= first), 0.0, -1e30).astype(jnp.float32)


def diagonal_of(size):
    shape = (size, size)
    return lax.broadcasted_iota(jnp.int32, shape, 0) == lax.broadcasted_iota(jnp.int32, shape, 1)


def as_column(row, diagonal):
    return jnp.sum(jnp.where(diagonal, row, jnp.zeros_like(row)), axis=1, keepdims=True)


def lanes_of(group, size):
    return slice(group * size, (group + 1) * size)


def group_rows(refs, group, size):
    return jnp.concatenate([ref[:, lanes_of(group, size)] for ref in reversed(refs)], axis=0)


def stacked(ref, group, per_group, size):
    heads = range(group * per_group, (group + 1) * per_group)
    return jnp.concatenate([ref[:, lanes_of(h, size)] for h in heads], axis=0)


def own_kernel(back, kv_count, *refs):
    hbm, targets, refs = refs[:10], refs[10:19], refs[19:]
    query_ref, key_ref, value_ref = targets[:3]
    qt_ref, raised_ref, sum_ref, stat_ref, bias_ref, doc_ref, sems = refs
    targets = (doc_ref,) + tuple(targets)
    tok_dev, head_size = query_ref.shape[0], key_ref.shape[1] // kv_count
    per_group = query_ref.shape[1] // head_size // kv_count
    rank = lax.axis_index("seq")
    scale = head_size**-0.5
    copies = [
        pltpu.make_async_copy(source, target, sems.at[at])
        for at, (source, target) in enumerate(zip(hbm, targets))
    ]
    for copy in copies:
        copy.start()
    copies[0].wait()
    bias_ref[...] = block_bias(doc_ref, rank, tok_dev, rank - back, back)
    bias = jnp.tile(block_bias(doc_ref, rank, tok_dev, rank, 1), (1, per_group))
    for copy in copies[1:4]:
        copy.wait()
    for group in range(kv_count):
        for at in range(per_group):
            tile = query_ref[:, lanes_of(group * per_group + at, head_size)]
            qt_ref[group, :, lanes_of(at, tok_dev)] = tile.T
        scores = dot(key_ref[:, lanes_of(group, head_size)], qt_ref[group], 1, 0)
        scores = scores * scale + bias
        top = jnp.max(scores, axis=0, keepdims=True)
        raised = jnp.exp(scores - top)
        raised_ref[group] = raised
        stat_ref[0, group : group + 1, :] = top
        stat_ref[1, group : group + 1, :] = jnp.sum(raised, axis=0, keepdims=True)
        sum_ref[group] = dot(
            value_ref[:, lanes_of(group, head_size)], raised.astype(jnp.bfloat16), 0, 0
        )
    for copy in copies[4:]:
        copy.wait()


def source_kernel(seq_count, source_ref, *refs):
    row_refs, out_ref = refs[:-1], refs[-1]
    tok_dev = out_ref.shape[1]
    rank = lax.axis_index("seq")
    diagonal = diagonal_of(tok_dev)
    places = lax.broadcasted_iota(jnp.int32, (tok_dev, tok_dev), 0)
    own = source_ref[:, pl.ds(pl.multiple_of(rank * tok_dev, tok_dev), tok_dev)]
    found = [jnp.zeros((1, tok_dev), jnp.float32)] * 2
    for at in range(seq_count):
        chosen = places + (rank ^ at) * tok_dev == own
        for kind in range(2):
            column = as_column(row_refs[kind * seq_count + at][...], diagonal)
            found[kind] = found[kind] + jnp.sum(
                jnp.where(chosen, column, 0.0), axis=0, keepdims=True
            )
    for kind in range(2):
        out_ref[kind : kind + 1, :] = found[kind]


def readout_terms(row, out_ref, whole_ref, relay):
    kv_count, _, wide = out_ref.shape
    tok_dev = row.shape[1]
    per_group = wide // tok_dev
    high = row.astype(jnp.bfloat16).astype(jnp.float32)
    middle = (row - high).astype(jnp.bfloat16).astype(jnp.float32)
    low = row - high - middle
    places = lax.broadcasted_iota(jnp.int32, (16, tok_dev), 0)
    rows = jnp.where(
        places == 0, high, jnp.where(places == 1, middle, jnp.where(places == 2, low, 0.0))
    ).astype(jnp.bfloat16)
    for group in range(kv_count):
        for at in range(per_group):
            h = group * per_group + at
            terms = dot(rows, out_ref[group, :, lanes_of(at, tok_dev)], 1, 1)
            place = h
            if relay:
                chunk = h // (kv_count * per_group // 4)
                place += ((chunk % 2) * 2 + chunk // 2 - chunk) * (kv_count * per_group // 4)
            whole_ref[place : place + 1, :] = jnp.sum(terms, axis=0, keepdims=True)


def forward_kernel(back, kv_count, relay, bit, *refs):
    bias_ref, now_ref, base_ref, readout_ref, qt_ref, sum_ref, stat_ref, upper_ref = refs[:8]
    key_refs, value_refs = refs[8 : 8 + back + relay], refs[8 + back + relay : 8 + 2 * (back + relay)]
    refs = refs[8 + 2 * (back + relay) :]
    rows_ref, raised_ref, out_ref, cot_ref, norm_ref, near_key_ref, near_value_ref = refs[:7]
    keep_ref, send_ref = refs[7:9]
    grad_value_refs, whole_ref = refs[9:-1], refs[-1]
    tok_dev = upper_ref.shape[0]
    head_count, head_size = readout_ref.shape
    per_group = head_count // kv_count
    scale = head_size**-0.5
    for near_ref, others in ((near_key_ref, key_refs), (near_value_ref, value_refs)):
        near_ref[...] = others[0][...]
        if relay:
            near_ref[...] = jnp.where(
                lax.axis_index("seq") % 2 == 1, others[0][...], others[1][...]
            )
    key_refs = (near_key_ref,) + tuple(key_refs[1 + relay :])
    value_refs = (near_value_ref,) + tuple(value_refs[1 + relay :])
    bias = jnp.tile(bias_ref[...], (1, per_group))
    total = base_ref[...]
    scales = []
    for group in range(kv_count):
        scores = dot(group_rows(key_refs, group, head_size), qt_ref[group], 1, 0)
        scores = scores * scale + bias
        own_top = stat_ref[0, group : group + 1, :]
        top = jnp.maximum(jnp.max(scores, axis=0, keepdims=True), own_top)
        raised = jnp.exp(scores - top)
        raised_ref[group] = raised
        shrink = jnp.exp(own_top - top)
        inverse = 1.0 / (
            jnp.sum(raised, axis=0, keepdims=True) + shrink * stat_ref[1, group : group + 1, :]
        )
        norm_ref[0, group : group + 1, :] = inverse
        norm_ref[1, group : group + 1, :] = shrink * inverse
        scales.append(inverse)
        out = dot(group_rows(value_refs, group, head_size), raised.astype(jnp.bfloat16), 0, 0)
        out = ((out + sum_ref[group] * shrink) * inverse).astype(jnp.bfloat16)
        out_ref[group] = out
        terms = dot(readout_ref[group * per_group : (group + 1) * per_group, :], out, 1, 0)
        for at in range(per_group):
            total = total + terms[at : at + 1, lanes_of(at, tok_dev)]
    value_cot = value_grad(total, now_ref[0:1, :], now_ref[1:2, :])
    rows_ref[0:1, :] = total
    rows_ref[1:2, :] = value_cot
    column = jnp.broadcast_to(as_column(value_cot, diagonal_of(tok_dev)), (tok_dev, head_size))
    for group in range(kv_count):
        cots = []
        for at in range(per_group):
            h = group * per_group + at
            cots.append(
                (
                    upper_ref[:, lanes_of(h, head_size)].astype(jnp.float32)
                    + column * readout_ref[h : h + 1, :].astype(jnp.float32)
                ).astype(jnp.bfloat16)
            )
        cot = jnp.concatenate(cots, axis=0)
        cot_ref[group] = cot
        weights = (raised_ref[group] * scales[group]).astype(jnp.bfloat16)
        grad_value = dot(weights, cot, 1, 0).astype(jnp.bfloat16)
        for step in range(1, back + 1):
            grad_value_refs[step - 1][:, lanes_of(group, head_size)] = grad_value[
                (back - step) * tok_dev : (back - step + 1) * tok_dev
            ]
    readout_terms(value_cot, out_ref, whole_ref, relay)
    halve(whole_ref, bit, keep_ref, send_ref)


def key_grad_kernel(back, kv_count, raised_ref, norm_ref, cot_ref, out_ref, query_ref, *refs):
    value_refs = refs[:back]
    delta_ref, ct_ref, grad_score_ref = refs[back : back + 3]
    grad_key_refs = refs[back + 3 :]
    tok_dev = query_ref.shape[0]
    head_size = out_ref.shape[1]
    per_group = query_ref.shape[1] // head_size // kv_count
    scale = head_size**-0.5
    for group in range(kv_count):
        for at in range(per_group):
            ct_ref[group, :, lanes_of(at, tok_dev)] = cot_ref[
                group, at * tok_dev : (at + 1) * tok_dev, :
            ].T
        turned = ct_ref[group]
        delta = jnp.sum(
            turned.astype(jnp.float32) * out_ref[group].astype(jnp.float32), axis=0, keepdims=True
        )
        delta_ref[group : group + 1, :] = delta
        grad_weights = dot(group_rows(value_refs, group, head_size), turned, 1, 0)
        grad_scores = raised_ref[group] * (
            (grad_weights - delta) * (norm_ref[0, group : group + 1, :] * scale)
        )
        grad_scores = grad_scores.astype(jnp.bfloat16)
        grad_score_ref[group] = grad_scores
        grad_key = dot(grad_scores, stacked(query_ref, group, per_group, head_size), 1, 0)
        grad_key = grad_key.astype(jnp.bfloat16)
        for step in range(1, back + 1):
            grad_key_refs[step - 1][:, lanes_of(group, head_size)] = grad_key[
                (back - step) * tok_dev : (back - step + 1) * tok_dev
            ]


def halve(whole_ref, bit, keep_ref, send_ref):
    rows = keep_ref.shape[0]
    mine = lax.rem(lax.div(lax.axis_index("seq"), bit), 2)
    keep_ref[...] = whole_ref[pl.ds(pl.multiple_of(mine * rows, rows), rows), :]
    send_ref[...] = whole_ref[pl.ds(pl.multiple_of((1 - mine) * rows, rows), rows), :]


def halve_kernel(bit, left_ref, right_ref, keep_ref, send_ref, whole_ref):
    whole_ref[...] = left_ref[...] + right_ref[...]
    halve(whole_ref, bit, keep_ref, send_ref)


def sum_kernel(left_ref, right_ref, out_ref):
    out_ref[...] = left_ref[...] + right_ref[...]


def relay_kernel(own_ref, far_ref, out_ref):
    passed = jnp.where(lax.axis_index("seq") % 2 == 1, far_ref[...].astype(jnp.float32), 0.0)
    out_ref[...] = (own_ref[...].astype(jnp.float32) + passed).astype(jnp.bfloat16)


def query_grad_kernel(back, kv_count, groups, *refs):
    raised_ref, norm_ref, delta_ref, cot_ref, ct_ref, score_ref, query_ref = refs[:7]
    key_refs, value_ref = refs[7 : 8 + back], refs[8 + back]
    grad_query_ref, own_key_ref, own_value_ref, piece_ref, sems = refs[-5:]
    tok_dev = query_ref.shape[0]
    head_size = ct_ref.shape[1]
    per_group = query_ref.shape[1] // head_size // kv_count
    scale = head_size**-0.5
    copies = []
    for at_group, group in enumerate(groups):
        lanes, own_lanes = lanes_of(group, head_size), lanes_of(at_group, head_size)
        weights = raised_ref[group] * norm_ref[1, group : group + 1, :]
        own_value_ref[:, own_lanes] = dot(weights.astype(jnp.bfloat16), cot_ref[group], 1, 0)
        grad_weights = dot(value_ref[:, lanes], ct_ref[group], 1, 0)
        grad_scores = weights * ((grad_weights - delta_ref[group : group + 1, :]) * scale)
        grad_scores = grad_scores.astype(jnp.bfloat16)
        own_key_ref[:, own_lanes] = dot(
            grad_scores, stacked(query_ref, group, per_group, head_size), 1, 0
        )
        scores = jnp.concatenate([score_ref[group], grad_scores], axis=0)
        grad_query = dot(group_rows(key_refs, group, head_size), scores, 0, 0)
        for at in range(per_group):
            piece_ref[at_group, :, lanes_of(at, head_size)] = grad_query[
                :, lanes_of(at, tok_dev)
            ].T.astype(jnp.bfloat16)
        copy = pltpu.make_async_copy(
            piece_ref.at[at_group],
            grad_query_ref.at[:, lanes_of(group, per_group * head_size)],
            sems.at[at_group],
        )
        copy.start()
        copies.append(copy)
    for copy in copies:
        copy.wait()


def combine_kernel(sections, relay, key_parts, *refs):
    own_key_refs, own_value_refs = refs[:sections], refs[sections : 2 * sections]
    rows_ref, left_ref, right_ref = refs[2 * sections : 2 * sections + 3]
    rest = refs[2 * sections + 3 : -4]
    key_refs, value_refs = rest[:key_parts], rest[key_parts:]
    values_ref, grad_key_ref, grad_value_ref, grad_readout_ref = refs[-4:]
    values_ref[...] = rows_ref[0:1, :]
    width = grad_key_ref.shape[1] // sections
    rank = lax.axis_index("seq")
    for section in range(sections):
        lanes = lanes_of(section, width)
        for own_refs, other_refs, out_ref in (
            (own_key_refs, key_refs, grad_key_ref),
            (own_value_refs, value_refs, grad_value_ref),
        ):
            total = own_refs[section][...]
            for at, other in enumerate(other_refs):
                term = other[:, lanes].astype(jnp.float32)
                if relay and at == 1:
                    term = jnp.where(rank % 2 == 0, term, 0.0)
                if relay and at == 2:
                    term = jnp.where(rank == 1, term, 0.0)
                total = total + term
            out_ref[:, lanes] = total.astype(jnp.bfloat16)
    total = left_ref[...] + right_ref[...]
    wide, own_size = total.shape[1], grad_readout_ref.shape[1]
    shift = lax.rem(wide - lax.axis_index("dp") * own_size, wide)
    grad_readout_ref[...] = pltpu.roll(total, shift, 1)[:, :own_size]


def on_device(
    queries,
    key_heads,
    value_heads,
    upper_cotangent,
    readout,
    base_value,
    old_values,
    returns,
    source_index,
    doc_lengths,
):
    seq_count = lax.axis_size("seq")
    dp_count = lax.axis_size("dp")
    tok_dev, _ = queries.shape
    head_count, head_size = readout.shape
    kv_width = key_heads.shape[1]
    kv_count = kv_width // head_size
    per_group = head_count // kv_count
    wide = per_group * tok_dev
    own_heads, own_size = head_count // seq_count, head_size // dp_count
    longest = tok_dev * seq_count // 2
    back = min(seq_count - 1, (longest - 1 + tok_dev - 1) // tok_dev)
    span = (back + 1) * tok_dev
    relay = seq_count == 4 and back == 2
    sections = 2

    def send(array, pairs, axis="seq"):
        return lax.ppermute(array, axis, pairs)

    def swap(array, bit, axis="seq"):
        return send(array, [(i, i ^ bit) for i in range(lax.axis_size(axis))], axis)

    def rotate(array, shift):
        return send(array, [(i, (i + shift) % seq_count) for i in range(seq_count)])

    relay_pairs = [(0, 0), (1, 1), (2, 3), (3, 2)]
    diagonal_pairs = [(0, 0), (1, 2), (2, 1), (3, 3)]

    vmem = pl.BlockSpec(memory_space=pltpu.VMEM)
    hbm = pl.BlockSpec(memory_space=pltpu.HBM)
    f32, bf16 = jnp.float32, jnp.bfloat16
    room = 8 + (kv_count * wide * span * 4 >> 20)
    unit = 2 * head_count * tok_dev * tok_dev * head_size

    def call(kernel, outs, args, megabytes=4, flops=1000, **more):
        more.setdefault("in_specs", [vmem] * len(args))
        more.setdefault("out_specs", [vmem] * len(outs))
        args = [
            pltpu.with_memory_space_constraint(arg, pltpu.HBM) if spec is hbm else arg
            for arg, spec in zip(args, more["in_specs"])
        ]
        return pl.pallas_call(
            kernel,
            out_shape=[jax.ShapeDtypeStruct(*out) for out in outs],
            compiler_params=pltpu.CompilerParams(vmem_limit_bytes=megabytes << 20),
            cost_estimate=pl.CostEstimate(
                flops=flops, bytes_accessed=flops // 1000, transcendentals=0
            ),
            **more,
        )(*args)

    def swap_rows(at):
        return [swap(array, at).reshape(1, tok_dev) for array in (old_values, returns)]

    keys, vals = [], []
    if relay:
        far_rows = swap_rows(2)
        value_far = swap(value_heads, 2)
        key_far = swap(key_heads, 2)
        near_rows = swap_rows(1)
        value_near = swap(value_heads, 1)
        key_near = swap(key_heads, 1)
        seen = [near_rows, far_rows, swap_rows(3)]
    else:
        seen = [swap_rows(at) for at in range(1, seq_count)]
        for step in range(1, back + 1):
            keys.append(rotate(key_heads, step))
            vals.append(rotate(value_heads, step))

    small = ((1, tok_dev), f32)
    outs = call(
        functools.partial(own_kernel, back, kv_count),
        [
            (queries.shape, bf16),
            (key_heads.shape, bf16),
            (value_heads.shape, bf16),
            (upper_cotangent.shape, bf16),
            (readout.shape, bf16),
            small,
            (source_index.shape, jnp.int32),
            small,
            small,
            ((kv_count, head_size, wide), bf16),
            ((kv_count, tok_dev, wide), f32),
            ((kv_count, head_size, wide), f32),
            ((2, kv_count, wide), f32),
            ((back * tok_dev, tok_dev), f32),
        ],
        [
            doc_lengths,
            queries,
            key_heads,
            value_heads,
            upper_cotangent,
            readout,
            base_value.reshape(1, tok_dev),
            source_index,
            old_values.reshape(1, tok_dev),
            returns.reshape(1, tok_dev),
        ],
        room,
        2 * unit,
        in_specs=[hbm] * 10,
        scratch_shapes=[
            pltpu.SMEM(doc_lengths.shape, jnp.int32),
            pltpu.SemaphoreType.DMA((10,)),
        ],
    )
    query_here, key_here, value_here, upper_here, readout_here, base_here = outs[:6]
    source_here, old_here, return_here = outs[6:9]
    turned_query, own_raised, own_sum, own_stat, bias = outs[9:]
    if relay:
        value_relay = send(value_far, relay_pairs)
        key_relay = send(key_heads, diagonal_pairs)
        keys = [key_near, key_relay, key_far]
        vals = [value_near, value_relay, value_far]
    (now,) = call(
        functools.partial(source_kernel, seq_count),
        [((2, tok_dev), f32)],
        [source_here, old_here]
        + [rows[0] for rows in seen]
        + [return_here]
        + [rows[1] for rows in seen],
        8,
    )
    bit = seq_count // 2 if not relay else 1
    size = head_count // 2
    outs = call(
        functools.partial(forward_kernel, back, kv_count, relay, 1 if relay else bit),
        [
            ((2, tok_dev), f32),
            ((kv_count, back * tok_dev, wide), f32),
            ((kv_count, head_size, wide), bf16),
            ((kv_count, wide, head_size), bf16),
            ((2, kv_count, wide), f32),
            (key_heads.shape, bf16),
            (key_heads.shape, bf16),
            ((size, head_size), f32),
            ((size, head_size), f32),
        ]
        + [(key_heads.shape, bf16)] * back,
        [bias, now, base_here, readout_here, turned_query, own_sum, own_stat, upper_here]
        + keys
        + vals,
        room,
        3 * back * unit,
        scratch_shapes=[pltpu.VMEM((head_count, head_size), f32)],
    )
    rows, raised, out, cot, norm, near_key, near_value, keep, away = outs[:9]
    grad_value = outs[9:]
    keys, vals = [near_key] + keys[1 + relay :], [near_value] + vals[1 + relay :]
    far = swap(away, bit)
    if relay:
        value_back = [swap(grad_value[0], 1)]
    else:
        value_back = [rotate(grad_value[step - 1], -step) for step in range(1, back + 1)]
    outs = call(
        functools.partial(key_grad_kernel, back, kv_count),
        [
            ((kv_count, wide), f32),
            ((kv_count, head_size, wide), bf16),
            ((kv_count, back * tok_dev, wide), bf16),
        ]
        + [(key_heads.shape, bf16)] * back,
        [raised, norm, cot, out, query_here] + vals,
        room,
        2 * back * unit,
    )
    delta, turned_cot, grad_scores = outs[:3]
    grad_key = outs[3:]
    bits = [2] if relay else [1 << at for at in range(seq_count.bit_length() - 1)][-2::-1]
    for bit in bits:
        size //= 2
        keep, away = call(
            functools.partial(halve_kernel, bit),
            [((size, head_size), f32)] * 2,
            [keep, far],
            scratch_shapes=[pltpu.VMEM((2 * size, head_size), f32)],
        )
        far = swap(away, bit)
    if relay:
        key_back = [swap(grad_key[1], 2), swap(grad_key[0], 1)]
    else:
        key_back = [rotate(grad_key[step - 1], -step) for step in range(1, back + 1)]

    def spread(left, right, bit):
        (total,) = call(sum_kernel, [((own_heads, head_size), f32)], [left, right])
        return total, swap(total, bit, "dp")

    def query_part(section, base):
        groups = range(section * kv_count // sections, (section + 1) * kv_count // sections)
        args = [own_raised, norm, delta, cot, turned_cot, grad_scores, query_here, key_here]
        args += keys + [value_here]
        aliases = {} if base is None else {len(args): 0}
        args += [] if base is None else [base]
        width = kv_width // sections
        return call(
            functools.partial(query_grad_kernel, back, kv_count, groups),
            [(queries.shape, bf16), ((tok_dev, width), f32), ((tok_dev, width), f32)],
            args,
            room,
            (4 + back) * unit // sections,
            in_specs=[vmem] * (9 + back) + [hbm] * len(aliases),
            out_specs=[hbm, vmem, vmem],
            scratch_shapes=[
                pltpu.VMEM((len(groups), tok_dev, wide // tok_dev * head_size), bf16),
                pltpu.SemaphoreType.DMA((len(groups),)),
            ],
            input_output_aliases=aliases,
        )

    bits = [1 << at for at in range(dp_count.bit_length() - 1)]
    keep, far = spread(keep, far, bits[0])
    if relay:
        key_back.append(send(grad_key[0], diagonal_pairs))
        (passed,) = call(relay_kernel, [(key_heads.shape, bf16)], [grad_value[1], value_back[0]])
        value_back.insert(0, swap(passed, 2))
    own_keys, own_values = [], []
    grad_queries = None
    for section in range(sections):
        keep, far = spread(keep, far, bits[1 + section])
        grad_queries, own_key, own_value = query_part(section, grad_queries)
        own_keys.append(own_key)
        own_values.append(own_value)
    for bit in bits[1 + sections :]:
        keep, far = spread(keep, far, bit)
    new_values, grad_key_heads, grad_value_heads, grad_readout = call(
        functools.partial(combine_kernel, sections, relay, len(key_back)),
        [small, (key_heads.shape, bf16), (key_heads.shape, bf16), ((own_heads, own_size), f32)],
        own_keys + own_values + [rows, keep, far] + key_back + value_back,
        8,
        unit // 100,
    )
    return (
        new_values.reshape(tok_dev),
        grad_queries,
        grad_key_heads,
        grad_value_heads,
        grad_readout,
    )


def solution(mesh):
    return jax.shard_map(
        on_device,
        mesh=mesh,
        in_specs=(
            P(("dp", "seq"), None),
            P(("dp", "seq"), None),
            P(("dp", "seq"), None),
            P(("dp", "seq"), None),
            P(),
            P(("dp", "seq")),
            P(("dp", "seq")),
            P(("dp", "seq")),
            P("dp", None),
            P("dp", None),
        ),
        out_specs=(
            P(("dp", "seq")),
            P(("dp", "seq"), None),
            P(("dp", "seq"), None),
            P(("dp", "seq"), None),
            P("seq", "dp"),
        ),
        check_vma=False,
    )
```

```python
import functools

import jax
import jax.numpy as jnp
from jax import lax
from jax.experimental import pallas as pl
from jax.experimental.pallas import tpu as pltpu
from jax.sharding import PartitionSpec as P


clip_range = 0.2
smooth_width = 0.1
loss_scale = 16.0


def value_grad(values, old_now, return_now):
    ratio = jnp.tanh((values - old_now) / clip_range)
    clipped = old_now + clip_range * ratio
    plain_gap = values - return_now
    clip_gap = clipped - return_now
    mixing = jax.nn.sigmoid((plain_gap * plain_gap - clip_gap * clip_gap) / smooth_width)
    return loss_scale * (mixing * plain_gap + (1.0 - mixing) * clip_gap * (1.0 - ratio * ratio))


def dot(left, right, left_dim, right_dim):
    return lax.dot_general(
        left,
        right,
        (((left_dim,), (right_dim,)), ((), ())),
        preferred_element_type=jnp.float32,
    )


def block_bias(doc_ref, rank, tok_dev, key_block, blocks):
    shape = (blocks * tok_dev, tok_dev)
    keys = lax.broadcasted_iota(jnp.int32, shape, 0) + key_block * tok_dev
    places = lax.broadcasted_iota(jnp.int32, shape, 1) + rank * tok_dev
    first = jnp.zeros(shape, jnp.int32)
    start = 0
    for doc in range(doc_ref.shape[1] - 1):
        size = doc_ref[0, doc]
        start = start + size
        first = first + jnp.where(places >= start, size, 0)
    return jnp.where((keys <= places) & (keys >= first), 0.0, -1e30).astype(jnp.float32)


def diagonal_of(size):
    shape = (size, size)
    return lax.broadcasted_iota(jnp.int32, shape, 0) == lax.broadcasted_iota(jnp.int32, shape, 1)


def as_column(row, diagonal):
    return jnp.sum(jnp.where(diagonal, row, jnp.zeros_like(row)), axis=1, keepdims=True)


def lanes_of(group, size):
    return slice(group * size, (group + 1) * size)


def group_rows(refs, group, size):
    return jnp.concatenate([ref[:, lanes_of(group, size)] for ref in reversed(refs)], axis=0)


def stacked(ref, group, per_group, size):
    heads = range(group * per_group, (group + 1) * per_group)
    return jnp.concatenate([ref[:, lanes_of(h, size)] for h in heads], axis=0)


def thirds(array):
    high = array.astype(jnp.bfloat16).astype(jnp.float32)
    middle = (array - high).astype(jnp.bfloat16).astype(jnp.float32)
    return high, middle, array - high - middle


def pack_kernel(value_hbm, old_hbm, return_hbm, pack_ref, old_ref, return_ref, sems):
    tok_dev = old_ref.shape[1]
    copies = [
        pltpu.make_async_copy(old_hbm, old_ref, sems.at[0]),
        pltpu.make_async_copy(return_hbm, return_ref, sems.at[1]),
        pltpu.make_async_copy(value_hbm, pack_ref.at[0:tok_dev, :], sems.at[2]),
    ]
    for copy in copies:
        copy.start()
    for copy in copies[:2]:
        copy.wait()
    places = lax.broadcasted_iota(jnp.int32, (16, tok_dev), 0)
    tile = jnp.zeros((16, tok_dev), jnp.float32)
    for at, third in enumerate(thirds(old_ref[...]) + thirds(return_ref[...])):
        tile = jnp.where(places == at, third, tile)
    pack_ref[tok_dev:, :] = jnp.zeros((16, pack_ref.shape[1]), jnp.bfloat16)
    pack_ref[tok_dev:, 0:tok_dev] = tile.astype(jnp.bfloat16)
    copies[2].wait()


def own_kernel(back, kv_count, *refs):
    hbm, targets, refs = refs[:10], refs[10:19], refs[19:]
    query_ref, key_ref, value_ref = targets[:3]
    qt_ref, raised_ref, sum_ref, stat_ref, bias_ref, doc_ref, sems = refs
    targets = (doc_ref,) + tuple(targets)
    tok_dev, head_size = query_ref.shape[0], key_ref.shape[1] // kv_count
    per_group = query_ref.shape[1] // head_size // kv_count
    rank = lax.axis_index("seq")
    scale = head_size**-0.5
    copies = [
        pltpu.make_async_copy(source, target, sems.at[at])
        for at, (source, target) in enumerate(zip(hbm, targets))
    ]
    for copy in copies:
        copy.start()
    copies[0].wait()
    bias_ref[...] = block_bias(doc_ref, rank, tok_dev, rank - back, back)
    bias = jnp.tile(block_bias(doc_ref, rank, tok_dev, rank, 1), (1, per_group))
    for copy in copies[1:4]:
        copy.wait()
    for group in range(kv_count):
        for at in range(per_group):
            tile = query_ref[:, lanes_of(group * per_group + at, head_size)]
            qt_ref[group, :, lanes_of(at, tok_dev)] = tile.T
        scores = dot(key_ref[:, lanes_of(group, head_size)], qt_ref[group], 1, 0)
        scores = scores * scale + bias
        top = jnp.max(scores, axis=0, keepdims=True)
        raised = jnp.exp(scores - top)
        raised_ref[group] = raised
        stat_ref[0, group : group + 1, :] = top
        stat_ref[1, group : group + 1, :] = jnp.sum(raised, axis=0, keepdims=True)
        sum_ref[group] = dot(
            value_ref[:, lanes_of(group, head_size)], raised.astype(jnp.bfloat16), 0, 0
        )
    for copy in copies[4:]:
        copy.wait()


def source_kernel(seq_count, relay, source_ref, *refs):
    row_refs, out_ref = refs[:-1], refs[-1]
    tok_dev = out_ref.shape[1]
    rank = lax.axis_index("seq")
    diagonal = diagonal_of(tok_dev)
    places = lax.broadcasted_iota(jnp.int32, (tok_dev, tok_dev), 0)
    own = source_ref[:, pl.ds(pl.multiple_of(rank * tok_dev, tok_dev), tok_dev)]
    found = [jnp.zeros((1, tok_dev), jnp.float32)] * 2
    for at in range(seq_count):
        chosen = places + (rank ^ at) * tok_dev == own
        for kind in range(2):
            if relay:
                tile = row_refs[at][tok_dev:, 0:tok_dev].astype(jnp.float32)
                row = tile[3 * kind : 3 * kind + 1] + tile[3 * kind + 1 : 3 * kind + 2]
                row = row + tile[3 * kind + 2 : 3 * kind + 3]
            else:
                row = row_refs[kind * seq_count + at][...]
            column = as_column(row, diagonal)
            found[kind] = found[kind] + jnp.sum(
                jnp.where(chosen, column, 0.0), axis=0, keepdims=True
            )
    for kind in range(2):
        out_ref[kind : kind + 1, :] = found[kind]


def readout_terms(row, out_ref, whole_ref, relay):
    kv_count, _, wide = out_ref.shape
    tok_dev = row.shape[1]
    per_group = wide // tok_dev
    high, middle, low = thirds(row)
    places = lax.broadcasted_iota(jnp.int32, (16, tok_dev), 0)
    rows = jnp.where(
        places == 0, high, jnp.where(places == 1, middle, jnp.where(places == 2, low, 0.0))
    ).astype(jnp.bfloat16)
    for group in range(kv_count):
        for at in range(per_group):
            h = group * per_group + at
            terms = dot(rows, out_ref[group, :, lanes_of(at, tok_dev)], 1, 1)
            place = h
            if relay:
                chunk = h // (kv_count * per_group // 4)
                place += ((chunk % 2) * 2 + chunk // 2 - chunk) * (kv_count * per_group // 4)
            whole_ref[place : place + 1, :] = jnp.sum(terms, axis=0, keepdims=True)


def forward_kernel(back, kv_count, relay, bit, *refs):
    bias_ref, now_ref, base_ref, readout_ref, qt_ref, sum_ref, stat_ref, upper_ref = refs[:8]
    key_refs, value_refs = refs[8 : 8 + back], refs[8 + back : 8 + 2 * back + relay]
    refs = refs[8 + 2 * back + relay :]
    rows_ref, raised_ref, out_ref, cot_ref, norm_ref, near_ref, keep_ref = refs[:7]
    grad_value_refs, send_ref, whole_ref = refs[7:-2], refs[-2], refs[-1]
    tok_dev = upper_ref.shape[0]
    head_count, head_size = readout_ref.shape
    per_group = head_count // kv_count
    scale = head_size**-0.5
    near_ref[...] = value_refs[0][0:tok_dev, :]
    if relay:
        direct, passed = value_refs[0][0:tok_dev, :], value_refs[1][0:tok_dev, :]
        near_ref[...] = jnp.where(lax.axis_index("seq") % 2 == 1, direct, passed)
    value_refs = (near_ref,) + tuple(ref.at[0:tok_dev, :] for ref in value_refs[1 + relay :])
    bias = jnp.tile(bias_ref[...], (1, per_group))
    total = base_ref[...]
    scales = []
    for group in range(kv_count):
        scores = dot(group_rows(key_refs, group, head_size), qt_ref[group], 1, 0)
        scores = scores * scale + bias
        own_top = stat_ref[0, group : group + 1, :]
        top = jnp.maximum(jnp.max(scores, axis=0, keepdims=True), own_top)
        raised = jnp.exp(scores - top)
        raised_ref[group] = raised
        shrink = jnp.exp(own_top - top)
        inverse = 1.0 / (
            jnp.sum(raised, axis=0, keepdims=True) + shrink * stat_ref[1, group : group + 1, :]
        )
        norm_ref[0, group : group + 1, :] = inverse
        norm_ref[1, group : group + 1, :] = shrink * inverse
        scales.append(inverse)
        out = dot(group_rows(value_refs, group, head_size), raised.astype(jnp.bfloat16), 0, 0)
        out = ((out + sum_ref[group] * shrink) * inverse).astype(jnp.bfloat16)
        out_ref[group] = out
        terms = dot(readout_ref[group * per_group : (group + 1) * per_group, :], out, 1, 0)
        for at in range(per_group):
            total = total + terms[at : at + 1, lanes_of(at, tok_dev)]
    value_cot = value_grad(total, now_ref[0:1, :], now_ref[1:2, :])
    rows_ref[0:1, :] = total
    rows_ref[1:2, :] = value_cot
    column = jnp.broadcast_to(as_column(value_cot, diagonal_of(tok_dev)), (tok_dev, head_size))
    for group in range(kv_count):
        cots = []
        for at in range(per_group):
            h = group * per_group + at
            cots.append(
                (
                    upper_ref[:, lanes_of(h, head_size)].astype(jnp.float32)
                    + column * readout_ref[h : h + 1, :].astype(jnp.float32)
                ).astype(jnp.bfloat16)
            )
        cot = jnp.concatenate(cots, axis=0)
        cot_ref[group] = cot
        weights = (raised_ref[group] * scales[group]).astype(jnp.bfloat16)
        grad_value = dot(weights, cot, 1, 0).astype(jnp.bfloat16)
        for step in range(1, back + 1):
            grad_value_refs[step - 1][0:tok_dev, lanes_of(group, head_size)] = grad_value[
                (back - step) * tok_dev : (back - step + 1) * tok_dev
            ]
    readout_terms(value_cot, out_ref, whole_ref, relay)
    halve(whole_ref, bit, keep_ref, send_ref)
    if relay:
        pack_ref = grad_value_refs[0]
        for at, third in enumerate(thirds(send_ref[...])):
            pack_ref[tok_dev:, lanes_of(at, head_size)] = third.astype(jnp.bfloat16)
        left = 3 * head_size
        pack_ref[tok_dev:, left:] = jnp.zeros((16, pack_ref.shape[1] - left), jnp.bfloat16)


def key_grad_kernel(back, kv_count, raised_ref, norm_ref, cot_ref, out_ref, query_ref, *refs):
    tok_dev = query_ref.shape[0]
    value_refs = [ref.at[0:tok_dev, :] for ref in refs[:back]]
    delta_ref, ct_ref, grad_score_ref = refs[back : back + 3]
    grad_key_refs = refs[back + 3 :]
    tok_dev = query_ref.shape[0]
    head_size = out_ref.shape[1]
    per_group = query_ref.shape[1] // head_size // kv_count
    scale = head_size**-0.5
    for group in range(kv_count):
        for at in range(per_group):
            ct_ref[group, :, lanes_of(at, tok_dev)] = cot_ref[
                group, at * tok_dev : (at + 1) * tok_dev, :
            ].T
        turned = ct_ref[group]
        delta = jnp.sum(
            turned.astype(jnp.float32) * out_ref[group].astype(jnp.float32), axis=0, keepdims=True
        )
        delta_ref[group : group + 1, :] = delta
        grad_weights = dot(group_rows(value_refs, group, head_size), turned, 1, 0)
        grad_scores = raised_ref[group] * (
            (grad_weights - delta) * (norm_ref[0, group : group + 1, :] * scale)
        )
        grad_scores = grad_scores.astype(jnp.bfloat16)
        grad_score_ref[group] = grad_scores
        grad_key = dot(grad_scores, stacked(query_ref, group, per_group, head_size), 1, 0)
        grad_key = grad_key.astype(jnp.bfloat16)
        for step in range(1, back + 1):
            grad_key_refs[step - 1][:, lanes_of(group, head_size)] = grad_key[
                (back - step) * tok_dev : (back - step + 1) * tok_dev
            ]


def halve(whole_ref, bit, keep_ref, send_ref):
    rows = keep_ref.shape[0]
    mine = lax.rem(lax.div(lax.axis_index("seq"), bit), 2)
    keep_ref[...] = whole_ref[pl.ds(pl.multiple_of(mine * rows, rows), rows), :]
    send_ref[...] = whole_ref[pl.ds(pl.multiple_of((1 - mine) * rows, rows), rows), :]


def halve_kernel(bit, packed, left_ref, right_ref, keep_ref, send_ref, whole_ref):
    if packed:
        rows, width = left_ref.shape
        tile = right_ref[right_ref.shape[0] - rows :, :].astype(jnp.float32)
        right = tile[:, lanes_of(0, width)] + tile[:, lanes_of(1, width)]
        whole_ref[...] = left_ref[...] + (right + tile[:, lanes_of(2, width)])
    else:
        whole_ref[...] = left_ref[...] + right_ref[...]
    halve(whole_ref, bit, keep_ref, send_ref)


def sum_kernel(left_ref, right_ref, out_ref):
    out_ref[...] = left_ref[...] + right_ref[...]


def relay_kernel(own_ref, far_ref, out_ref):
    far = far_ref[0 : own_ref.shape[0], :].astype(jnp.float32)
    passed = jnp.where(lax.axis_index("seq") % 2 == 1, far, 0.0)
    out_ref[...] = (own_ref[...].astype(jnp.float32) + passed).astype(jnp.bfloat16)


def query_grad_kernel(back, kv_count, groups, *refs):
    raised_ref, norm_ref, delta_ref, cot_ref, ct_ref, score_ref, query_ref = refs[:7]
    key_refs, value_ref = refs[7 : 8 + back], refs[8 + back]
    grad_query_ref, own_key_ref, own_value_ref, piece_ref, sems = refs[-5:]
    tok_dev = query_ref.shape[0]
    head_size = ct_ref.shape[1]
    per_group = query_ref.shape[1] // head_size // kv_count
    scale = head_size**-0.5
    copies = []
    for at_group, group in enumerate(groups):
        lanes, own_lanes = lanes_of(group, head_size), lanes_of(at_group, head_size)
        weights = raised_ref[group] * norm_ref[1, group : group + 1, :]
        own_value_ref[:, own_lanes] = dot(weights.astype(jnp.bfloat16), cot_ref[group], 1, 0)
        grad_weights = dot(value_ref[:, lanes], ct_ref[group], 1, 0)
        grad_scores = weights * ((grad_weights - delta_ref[group : group + 1, :]) * scale)
        grad_scores = grad_scores.astype(jnp.bfloat16)
        own_key_ref[:, own_lanes] = dot(
            grad_scores, stacked(query_ref, group, per_group, head_size), 1, 0
        )
        scores = jnp.concatenate([score_ref[group], grad_scores], axis=0)
        grad_query = dot(group_rows(key_refs, group, head_size), scores, 0, 0)
        for at in range(per_group):
            piece_ref[at_group, :, lanes_of(at, head_size)] = grad_query[
                :, lanes_of(at, tok_dev)
            ].T.astype(jnp.bfloat16)
        copy = pltpu.make_async_copy(
            piece_ref.at[at_group],
            grad_query_ref.at[:, lanes_of(group, per_group * head_size)],
            sems.at[at_group],
        )
        copy.start()
        copies.append(copy)
    for copy in copies:
        copy.wait()


def combine_kernel(sections, relay, key_parts, *refs):
    own_key_refs, own_value_refs = refs[:sections], refs[sections : 2 * sections]
    rows_ref, left_ref, right_ref = refs[2 * sections : 2 * sections + 3]
    rest = refs[2 * sections + 3 : -4]
    key_refs, value_refs = rest[:key_parts], rest[key_parts:]
    values_ref, grad_key_ref, grad_value_ref, grad_readout_ref = refs[-4:]
    values_ref[...] = rows_ref[0:1, :]
    width = grad_key_ref.shape[1] // sections
    rank = lax.axis_index("seq")
    for section in range(sections):
        lanes = lanes_of(section, width)
        for own_refs, other_refs, out_ref in (
            (own_key_refs, key_refs, grad_key_ref),
            (own_value_refs, value_refs, grad_value_ref),
        ):
            total = own_refs[section][...]
            for at, other in enumerate(other_refs):
                term = other[0 : out_ref.shape[0], lanes].astype(jnp.float32)
                if relay and at == 1:
                    term = jnp.where(rank % 2 == 0, term, 0.0)
                total = total + term
            out_ref[:, lanes] = total.astype(jnp.bfloat16)
    total = left_ref[...] + right_ref[...]
    wide, own_size = total.shape[1], grad_readout_ref.shape[1]
    shift = lax.rem(wide - lax.axis_index("dp") * own_size, wide)
    grad_readout_ref[...] = pltpu.roll(total, shift, 1)[:, :own_size]


def on_device(
    queries,
    key_heads,
    value_heads,
    upper_cotangent,
    readout,
    base_value,
    old_values,
    returns,
    source_index,
    doc_lengths,
):
    seq_count = lax.axis_size("seq")
    dp_count = lax.axis_size("dp")
    tok_dev, _ = queries.shape
    head_count, head_size = readout.shape
    kv_width = key_heads.shape[1]
    kv_count = kv_width // head_size
    per_group = head_count // kv_count
    wide = per_group * tok_dev
    own_heads, own_size = head_count // seq_count, head_size // dp_count
    longest = tok_dev * seq_count // 2
    back = min(seq_count - 1, (longest - 1 + tok_dev - 1) // tok_dev)
    span = (back + 1) * tok_dev
    relay = seq_count == 4 and back == 2
    sections = 2

    def send(array, pairs, axis="seq"):
        return lax.ppermute(array, axis, pairs)

    def swap(array, bit, axis="seq"):
        return send(array, [(i, i ^ bit) for i in range(lax.axis_size(axis))], axis)

    def rotate(array, shift):
        return send(array, [(i, (i + shift) % seq_count) for i in range(seq_count)])

    vmem = pl.BlockSpec(memory_space=pltpu.VMEM)
    hbm = pl.BlockSpec(memory_space=pltpu.HBM)
    f32, bf16 = jnp.float32, jnp.bfloat16
    room = 8 + (kv_count * wide * span * 4 >> 20)
    unit = 2 * head_count * tok_dev * tok_dev * head_size

    def call(kernel, outs, args, megabytes=4, flops=1000, **more):
        more.setdefault("in_specs", [vmem] * len(args))
        more.setdefault("out_specs", [vmem] * len(outs))
        args = [
            pltpu.with_memory_space_constraint(arg, pltpu.HBM) if spec is hbm else arg
            for arg, spec in zip(args, more["in_specs"])
        ]
        return pl.pallas_call(
            kernel,
            out_shape=[jax.ShapeDtypeStruct(*out) for out in outs],
            compiler_params=pltpu.CompilerParams(vmem_limit_bytes=megabytes << 20),
            cost_estimate=pl.CostEstimate(
                flops=flops, bytes_accessed=flops // 1000, transcendentals=0
            ),
            **more,
        )(*args)

    def swap_rows(at):
        return [swap(array, at).reshape(1, tok_dev) for array in (old_values, returns)]

    small = ((1, tok_dev), f32)
    keys, vals = [], []
    if relay:
        (pack,) = call(
            pack_kernel,
            [((tok_dev + 16, kv_width), bf16)],
            [value_heads, old_values.reshape(1, tok_dev), returns.reshape(1, tok_dev)],
            in_specs=[hbm] * 3,
            scratch_shapes=[pltpu.VMEM(*small), pltpu.VMEM(*small), pltpu.SemaphoreType.DMA((3,))],
        )
        value_far = swap(pack, 2)
        value_near = swap(pack, 1)
        key_far = rotate(key_heads, 2)
        keys = [rotate(key_heads, 1), key_far]
        value_relay = swap(value_far, 1)
        vals = [value_near, value_relay, value_far]
    else:
        seen = [swap_rows(at) for at in range(1, seq_count)]
        for step in range(1, back + 1):
            keys.append(rotate(key_heads, step))
            vals.append(rotate(value_heads, step))
    outs = call(
        functools.partial(own_kernel, back, kv_count),
        [
            (queries.shape, bf16),
            (key_heads.shape, bf16),
            (value_heads.shape, bf16),
            (upper_cotangent.shape, bf16),
            (readout.shape, bf16),
            small,
            (source_index.shape, jnp.int32),
            small,
            small,
            ((kv_count, head_size, wide), bf16),
            ((kv_count, tok_dev, wide), f32),
            ((kv_count, head_size, wide), f32),
            ((2, kv_count, wide), f32),
            ((back * tok_dev, tok_dev), f32),
        ],
        [
            doc_lengths,
            queries,
            key_heads,
            value_heads,
            upper_cotangent,
            readout,
            base_value.reshape(1, tok_dev),
            source_index,
            old_values.reshape(1, tok_dev),
            returns.reshape(1, tok_dev),
        ],
        room,
        2 * unit,
        in_specs=[hbm] * 10,
        scratch_shapes=[
            pltpu.SMEM(doc_lengths.shape, jnp.int32),
            pltpu.SemaphoreType.DMA((10,)),
        ],
    )
    query_here, key_here, value_here, upper_here, readout_here, base_here = outs[:6]
    source_here, old_here, return_here = outs[6:9]
    turned_query, own_raised, own_sum, own_stat, bias = outs[9:]
    if relay:
        row_args = [pack, value_near, value_far, value_relay]
    else:
        row_args = [old_here] + [rows[0] for rows in seen]
        row_args += [return_here] + [rows[1] for rows in seen]
    (now,) = call(
        functools.partial(source_kernel, seq_count, relay),
        [((2, tok_dev), f32)],
        [source_here, *row_args],
        8,
    )
    bit = seq_count // 2 if not relay else 1
    size = head_count // 2
    outs = call(
        functools.partial(forward_kernel, back, kv_count, relay, 1 if relay else bit),
        [
            ((2, tok_dev), f32),
            ((kv_count, back * tok_dev, wide), f32),
            ((kv_count, head_size, wide), bf16),
            ((kv_count, wide, head_size), bf16),
            ((2, kv_count, wide), f32),
            (key_heads.shape, bf16),
            ((size, head_size), f32),
            ((tok_dev + 16 * relay, kv_width), bf16),
        ]
        + [(key_heads.shape, bf16)] * (back - 1)
        + [((size, head_size), f32)],
        [bias, now, base_here, readout_here, turned_query, own_sum, own_stat, upper_here]
        + keys
        + vals,
        room,
        3 * back * unit,
        scratch_shapes=[pltpu.VMEM((head_count, head_size), f32)],
    )
    rows, raised, out, cot, norm, near, keep = outs[:7]
    grad_value, away = outs[7:-1], outs[-1]
    vals = [near] + vals[1 + relay :]
    if not relay:
        far = swap(away, bit)
    if relay:
        far = swap(grad_value[0], 1)
        value_back = [far]
    else:
        value_back = [rotate(grad_value[step - 1], -step) for step in range(1, back + 1)]
    outs = call(
        functools.partial(key_grad_kernel, back, kv_count),
        [
            ((kv_count, wide), f32),
            ((kv_count, head_size, wide), bf16),
            ((kv_count, back * tok_dev, wide), bf16),
        ]
        + [(key_heads.shape, bf16)] * back,
        [raised, norm, cot, out, query_here] + vals,
        room,
        2 * back * unit,
    )
    delta, turned_cot, grad_scores = outs[:3]
    grad_key = outs[3:]
    bits = [2] if relay else [1 << at for at in range(seq_count.bit_length() - 1)][-2::-1]
    for bit in bits:
        size //= 2
        keep, away = call(
            functools.partial(halve_kernel, bit, relay),
            [((size, head_size), f32)] * 2,
            [keep, far],
            scratch_shapes=[pltpu.VMEM((2 * size, head_size), f32)],
        )
        far = swap(away, bit)
    if relay:
        key_back = [swap(grad_key[0], 1)]
    else:
        key_back = [rotate(grad_key[step - 1], -step) for step in range(1, back + 1)]

    def pass_on(own, parts):
        (passed,) = call(relay_kernel, [(key_heads.shape, bf16)], [own, parts[0]])
        parts.insert(0, swap(passed, 2))

    def spread(left, right, bit):
        (total,) = call(sum_kernel, [((own_heads, head_size), f32)], [left, right])
        return total, swap(total, bit, "dp")

    def query_part(section, base):
        groups = range(section * kv_count // sections, (section + 1) * kv_count // sections)
        args = [own_raised, norm, delta, cot, turned_cot, grad_scores, query_here, key_here]
        args += keys + [value_here]
        aliases = {} if base is None else {len(args): 0}
        args += [] if base is None else [base]
        width = kv_width // sections
        return call(
            functools.partial(query_grad_kernel, back, kv_count, groups),
            [(queries.shape, bf16), ((tok_dev, width), f32), ((tok_dev, width), f32)],
            args,
            room,
            (4 + back) * unit // sections,
            in_specs=[vmem] * (9 + back) + [hbm] * len(aliases),
            out_specs=[hbm, vmem, vmem],
            scratch_shapes=[
                pltpu.VMEM((len(groups), tok_dev, wide // tok_dev * head_size), bf16),
                pltpu.SemaphoreType.DMA((len(groups),)),
            ],
            input_output_aliases=aliases,
        )

    bits = [1 << at for at in range(dp_count.bit_length() - 1)]
    keep, far = spread(keep, far, bits[0])
    if relay:
        pass_on(grad_value[1], value_back)
        pass_on(grad_key[1], key_back)
    own_keys, own_values = [], []
    grad_queries = None
    for section in range(sections):
        keep, far = spread(keep, far, bits[1 + section])
        grad_queries, own_key, own_value = query_part(section, grad_queries)
        own_keys.append(own_key)
        own_values.append(own_value)
    for bit in bits[1 + sections :]:
        keep, far = spread(keep, far, bit)
    new_values, grad_key_heads, grad_value_heads, grad_readout = call(
        functools.partial(combine_kernel, sections, relay, len(key_back)),
        [small, (key_heads.shape, bf16), (key_heads.shape, bf16), ((own_heads, own_size), f32)],
        own_keys + own_values + [rows, keep, far] + key_back + value_back,
        8,
        unit // 100,
    )
    return (
        new_values.reshape(tok_dev),
        grad_queries,
        grad_key_heads,
        grad_value_heads,
        grad_readout,
    )


def solution(mesh):
    return jax.shard_map(
        on_device,
        mesh=mesh,
        in_specs=(
            P(("dp", "seq"), None),
            P(("dp", "seq"), None),
            P(("dp", "seq"), None),
            P(("dp", "seq"), None),
            P(),
            P(("dp", "seq")),
            P(("dp", "seq")),
            P(("dp", "seq")),
            P("dp", None),
            P("dp", None),
        ),
        out_specs=(
            P(("dp", "seq")),
            P(("dp", "seq"), None),
            P(("dp", "seq"), None),
            P(("dp", "seq"), None),
            P("seq", "dp"),
        ),
        check_vma=False,
    )
```

```python
import functools

import jax
import jax.numpy as jnp
from jax import lax
from jax.experimental import pallas as pl
from jax.experimental.pallas import tpu as pltpu
from jax.sharding import PartitionSpec as P


clip_range = 0.2
smooth_width = 0.1
loss_scale = 16.0


def value_grad(values, old_now, return_now):
    ratio = jnp.tanh((values - old_now) / clip_range)
    clipped = old_now + clip_range * ratio
    plain_gap = values - return_now
    clip_gap = clipped - return_now
    mixing = jax.nn.sigmoid((plain_gap * plain_gap - clip_gap * clip_gap) / smooth_width)
    return loss_scale * (mixing * plain_gap + (1.0 - mixing) * clip_gap * (1.0 - ratio * ratio))


def dot(left, right, left_dim, right_dim):
    return lax.dot_general(
        left,
        right,
        (((left_dim,), (right_dim,)), ((), ())),
        preferred_element_type=jnp.float32,
    )


def block_bias(doc_ref, rank, tok_dev, key_block, blocks):
    shape = (blocks * tok_dev, tok_dev)
    keys = lax.broadcasted_iota(jnp.int32, shape, 0) + key_block * tok_dev
    places = lax.broadcasted_iota(jnp.int32, shape, 1) + rank * tok_dev
    first = jnp.zeros(shape, jnp.int32)
    start = 0
    for doc in range(doc_ref.shape[1] - 1):
        size = doc_ref[0, doc]
        start = start + size
        first = first + jnp.where(places >= start, size, 0)
    return jnp.where((keys <= places) & (keys >= first), 0.0, -1e30).astype(jnp.float32)


def diagonal_of(size):
    shape = (size, size)
    return lax.broadcasted_iota(jnp.int32, shape, 0) == lax.broadcasted_iota(jnp.int32, shape, 1)


def as_column(row, diagonal):
    return jnp.sum(jnp.where(diagonal, row, jnp.zeros_like(row)), axis=1, keepdims=True)


def lanes_of(group, size):
    return slice(group * size, (group + 1) * size)


def group_rows(refs, group, size):
    return jnp.concatenate([ref[:, lanes_of(group, size)] for ref in reversed(refs)], axis=0)


def stacked(ref, group, per_group, size):
    heads = range(group * per_group, (group + 1) * per_group)
    return jnp.concatenate([ref[:, lanes_of(h, size)] for h in heads], axis=0)


def thirds(array):
    high = array.astype(jnp.bfloat16).astype(jnp.float32)
    middle = (array - high).astype(jnp.bfloat16).astype(jnp.float32)
    return high, middle, array - high - middle


def pack_kernel(value_hbm, old_hbm, return_hbm, pack_ref, pair_ref, old_ref, return_ref, sems):
    tok_dev = old_ref.shape[1]
    copies = [
        pltpu.make_async_copy(old_hbm, old_ref, sems.at[0]),
        pltpu.make_async_copy(return_hbm, return_ref, sems.at[1]),
        pltpu.make_async_copy(value_hbm, pack_ref.at[0:tok_dev, :], sems.at[2]),
    ]
    for copy in copies:
        copy.start()
    for copy in copies[:2]:
        copy.wait()
    places = lax.broadcasted_iota(jnp.int32, (16, tok_dev), 0)
    tile = jnp.zeros((16, tok_dev), jnp.float32)
    for at, third in enumerate(thirds(old_ref[...]) + thirds(return_ref[...])):
        tile = jnp.where(places == at, third, tile)
    pair_ref[0:1, :] = old_ref[...]
    pair_ref[1:2, :] = return_ref[...]
    pack_ref[tok_dev:, :] = jnp.zeros((16, pack_ref.shape[1]), jnp.bfloat16)
    pack_ref[tok_dev:, 0:tok_dev] = tile.astype(jnp.bfloat16)
    copies[2].wait()


def own_kernel(back, kv_count, *refs):
    hbm, targets, refs = refs[:10], refs[10:19], refs[19:]
    query_ref, key_ref, value_ref = targets[:3]
    qt_ref, raised_ref, sum_ref, stat_ref, bias_ref, doc_ref, sems = refs
    targets = (doc_ref,) + tuple(targets)
    tok_dev, head_size = query_ref.shape[0], key_ref.shape[1] // kv_count
    per_group = query_ref.shape[1] // head_size // kv_count
    rank = lax.axis_index("seq")
    scale = head_size**-0.5
    copies = [
        pltpu.make_async_copy(source, target, sems.at[at])
        for at, (source, target) in enumerate(zip(hbm, targets))
    ]
    for copy in copies:
        copy.start()
    copies[0].wait()
    bias_ref[...] = block_bias(doc_ref, rank, tok_dev, rank - back, back)
    bias = jnp.tile(block_bias(doc_ref, rank, tok_dev, rank, 1), (1, per_group))
    for copy in copies[1:4]:
        copy.wait()
    for group in range(kv_count):
        for at in range(per_group):
            tile = query_ref[:, lanes_of(group * per_group + at, head_size)]
            qt_ref[group, :, lanes_of(at, tok_dev)] = tile.T
        scores = dot(key_ref[:, lanes_of(group, head_size)], qt_ref[group], 1, 0)
        scores = scores * scale + bias
        top = jnp.max(scores, axis=0, keepdims=True)
        raised = jnp.exp(scores - top)
        raised_ref[group] = raised
        stat_ref[0, group : group + 1, :] = top
        stat_ref[1, group : group + 1, :] = jnp.sum(raised, axis=0, keepdims=True)
        sum_ref[group] = dot(
            value_ref[:, lanes_of(group, head_size)], raised.astype(jnp.bfloat16), 0, 0
        )
    for copy in copies[4:]:
        copy.wait()


def source_kernel(seq_count, relay, source_ref, *refs):
    row_refs, out_ref = refs[:-1], refs[-1]
    tok_dev = out_ref.shape[1]
    rank = lax.axis_index("seq")
    diagonal = diagonal_of(tok_dev)
    places = lax.broadcasted_iota(jnp.int32, (tok_dev, tok_dev), 0)
    own = source_ref[:, pl.ds(pl.multiple_of(rank * tok_dev, tok_dev), tok_dev)]
    found = [jnp.zeros((1, tok_dev), jnp.float32)] * 2
    for at in range(seq_count):
        owner = lax.rem(rank - at + seq_count, seq_count) if relay else rank ^ at
        chosen = places + owner * tok_dev == own
        for kind in range(2):
            if relay and at < seq_count - 1:
                tile = row_refs[at][tok_dev:, 0:tok_dev].astype(jnp.float32)
                row = tile[3 * kind : 3 * kind + 1] + tile[3 * kind + 1 : 3 * kind + 2]
                row = row + tile[3 * kind + 2 : 3 * kind + 3]
            elif relay:
                row = row_refs[at][kind : kind + 1, :]
            else:
                row = row_refs[kind * seq_count + at][...]
            column = as_column(row, diagonal)
            found[kind] = found[kind] + jnp.sum(
                jnp.where(chosen, column, 0.0), axis=0, keepdims=True
            )
    for kind in range(2):
        out_ref[kind : kind + 1, :] = found[kind]


def readout_terms(row, out_ref, whole_ref):
    kv_count, _, wide = out_ref.shape
    tok_dev = row.shape[1]
    per_group = wide // tok_dev
    high, middle, low = thirds(row)
    places = lax.broadcasted_iota(jnp.int32, (16, tok_dev), 0)
    rows = jnp.where(
        places == 0, high, jnp.where(places == 1, middle, jnp.where(places == 2, low, 0.0))
    ).astype(jnp.bfloat16)
    for group in range(kv_count):
        for at in range(per_group):
            h = group * per_group + at
            terms = dot(rows, out_ref[group, :, lanes_of(at, tok_dev)], 1, 1)
            whole_ref[h : h + 1, :] = jnp.sum(terms, axis=0, keepdims=True)


def forward_kernel(back, kv_count, relay, bit, *refs):
    bias_ref, now_ref, base_ref, readout_ref, qt_ref, sum_ref, stat_ref = refs[:7]
    key_refs, value_refs = refs[7 : 7 + back + relay], refs[7 + back + relay : 7 + 2 * back + relay]
    refs = refs[7 + 2 * back + relay :]
    rows_ref, raised_ref, out_ref, norm_ref, near_ref, keep_ref, send_ref, whole_ref = refs
    tok_dev = bias_ref.shape[1]
    head_count, head_size = readout_ref.shape
    per_group = head_count // kv_count
    scale = head_size**-0.5
    near_ref[...] = key_refs[0][...]
    if relay:
        near_ref[...] = jnp.where(
            lax.axis_index("seq") % 2 == 1, key_refs[0][...], key_refs[1][...]
        )
    key_refs = (near_ref,) + tuple(key_refs[1 + relay :])
    value_refs = [ref.at[0:tok_dev, :] for ref in value_refs]
    bias = jnp.tile(bias_ref[...], (1, per_group))
    total = base_ref[...]
    for group in range(kv_count):
        scores = dot(group_rows(key_refs, group, head_size), qt_ref[group], 1, 0)
        scores = scores * scale + bias
        own_top = stat_ref[0, group : group + 1, :]
        top = jnp.maximum(jnp.max(scores, axis=0, keepdims=True), own_top)
        raised = jnp.exp(scores - top)
        raised_ref[group] = raised
        shrink = jnp.exp(own_top - top)
        inverse = 1.0 / (
            jnp.sum(raised, axis=0, keepdims=True) + shrink * stat_ref[1, group : group + 1, :]
        )
        norm_ref[0, group : group + 1, :] = inverse
        norm_ref[1, group : group + 1, :] = shrink * inverse
        out = dot(group_rows(value_refs, group, head_size), raised.astype(jnp.bfloat16), 0, 0)
        out = ((out + sum_ref[group] * shrink) * inverse).astype(jnp.bfloat16)
        out_ref[group] = out
        terms = dot(readout_ref[group * per_group : (group + 1) * per_group, :], out, 1, 0)
        for at in range(per_group):
            total = total + terms[at : at + 1, lanes_of(at, tok_dev)]
    value_cot = value_grad(total, now_ref[0:1, :], now_ref[1:2, :])
    rows_ref[0:1, :] = total
    rows_ref[1:2, :] = value_cot
    readout_terms(value_cot, out_ref, whole_ref)
    halve(whole_ref, bit, keep_ref, send_ref)


def backward_kernel(back, kv_count, *refs):
    rows_ref, upper_ref, readout_ref, raised_ref, norm_ref, out_ref, query_ref = refs[:7]
    tok_dev = query_ref.shape[0]
    value_refs = [ref.at[0:tok_dev, :] for ref in refs[7 : 7 + back]]
    delta_ref, cot_ref, ct_ref, grad_score_ref = refs[7 + back : 11 + back]
    grad_refs = refs[11 + back :]
    head_count, head_size = readout_ref.shape
    per_group = head_count // kv_count
    scale = head_size**-0.5
    value_cot = rows_ref[1:2, :]
    column = jnp.broadcast_to(as_column(value_cot, diagonal_of(tok_dev)), (tok_dev, head_size))
    for group in range(kv_count):
        cots = []
        for at in range(per_group):
            h = group * per_group + at
            cot = (
                upper_ref[:, lanes_of(h, head_size)].astype(jnp.float32)
                + column * readout_ref[h : h + 1, :].astype(jnp.float32)
            ).astype(jnp.bfloat16)
            cots.append(cot)
            ct_ref[group, :, lanes_of(at, tok_dev)] = cot.T
        cot = jnp.concatenate(cots, axis=0)
        cot_ref[group] = cot
        turned = ct_ref[group]
        delta = jnp.sum(
            turned.astype(jnp.float32) * out_ref[group].astype(jnp.float32), axis=0, keepdims=True
        )
        delta_ref[group : group + 1, :] = delta
        weights = raised_ref[group] * norm_ref[0, group : group + 1, :]
        grad_value = dot(weights.astype(jnp.bfloat16), cot, 1, 0).astype(jnp.bfloat16)
        grad_weights = dot(group_rows(value_refs, group, head_size), turned, 1, 0)
        grad_scores = (weights * ((grad_weights - delta) * scale)).astype(jnp.bfloat16)
        grad_score_ref[group] = grad_scores
        grad_key = dot(grad_scores, stacked(query_ref, group, per_group, head_size), 1, 0)
        grad_key = grad_key.astype(jnp.bfloat16)
        for step in range(1, back + 1):
            block = slice((back - step) * tok_dev, (back - step + 1) * tok_dev)
            grad_refs[step - 1][:, lanes_of(group, head_size)] = grad_key[block]
            grad_refs[step - 1][:, lanes_of(kv_count + group, head_size)] = grad_value[block]


def halve(whole_ref, bit, keep_ref, send_ref):
    rows = keep_ref.shape[0]
    mine = lax.rem(lax.div(lax.axis_index("seq"), bit), 2)
    keep_ref[...] = whole_ref[pl.ds(pl.multiple_of(mine * rows, rows), rows), :]
    send_ref[...] = whole_ref[pl.ds(pl.multiple_of((1 - mine) * rows, rows), rows), :]


def halve_kernel(bit, left_ref, right_ref, keep_ref, send_ref, whole_ref):
    whole_ref[...] = left_ref[...] + right_ref[...]
    halve(whole_ref, bit, keep_ref, send_ref)


def sum_kernel(left_ref, right_ref, out_ref):
    out_ref[...] = left_ref[...] + right_ref[...]


def query_grad_kernel(back, kv_count, groups, *refs):
    raised_ref, norm_ref, delta_ref, cot_ref, ct_ref, score_ref, query_ref = refs[:7]
    key_refs, value_ref = refs[7 : 8 + back], refs[8 + back]
    piece_ref, own_key_ref, own_value_ref = refs[9 + back :]
    tok_dev = query_ref.shape[0]
    head_size = ct_ref.shape[1]
    per_group = query_ref.shape[1] // head_size // kv_count
    scale = head_size**-0.5
    for at_group, group in enumerate(groups):
        lanes, own_lanes = lanes_of(group, head_size), lanes_of(at_group, head_size)
        weights = raised_ref[group] * norm_ref[1, group : group + 1, :]
        own_value_ref[:, own_lanes] = dot(weights.astype(jnp.bfloat16), cot_ref[group], 1, 0)
        grad_weights = dot(value_ref[:, lanes], ct_ref[group], 1, 0)
        grad_scores = weights * ((grad_weights - delta_ref[group : group + 1, :]) * scale)
        grad_scores = grad_scores.astype(jnp.bfloat16)
        own_key_ref[:, own_lanes] = dot(
            grad_scores, stacked(query_ref, group, per_group, head_size), 1, 0
        )
        scores = jnp.concatenate([score_ref[group], grad_scores], axis=0)
        grad_query = dot(group_rows(key_refs, group, head_size), scores, 0, 0)
        for at in range(per_group):
            lanes = lanes_of(at_group * per_group + at, head_size)
            turned = grad_query[:, lanes_of(at, tok_dev)].T
            piece_ref[:, lanes] = turned.astype(jnp.bfloat16)


def combine_kernel(sections, *refs):
    own_refs, refs = refs[: 3 * sections], refs[3 * sections :]
    rows_ref, left_ref, right_ref = refs[:3]
    back_refs = refs[3:-6]
    values_ref, grad_query_ref, grad_key_ref, grad_value_ref, grad_readout_ref, sems = refs[-6:]
    copies, left = [], 0
    for section in range(sections):
        piece_ref = own_refs[3 * section]
        right = left + piece_ref.shape[1]
        target = grad_query_ref.at[:, left:right]
        copies.append(pltpu.make_async_copy(piece_ref, target, sems.at[section]))
        copies[-1].start()
        left = right
    values_ref[...] = rows_ref[0:1, :]
    for kind, out_ref in ((0, grad_key_ref), (1, grad_value_ref)):
        left = 0
        for section in range(sections):
            total = own_refs[3 * section + 1 + kind][...]
            right = left + total.shape[1]
            start = kind * out_ref.shape[1]
            for other in back_refs:
                total = total + other[:, start + left : start + right].astype(jnp.float32)
            out_ref[:, left:right] = total.astype(jnp.bfloat16)
            left = right
    total = left_ref[...] + right_ref[...]
    wide, own_size = total.shape[1], grad_readout_ref.shape[1]
    shift = lax.rem(wide - lax.axis_index("dp") * own_size, wide)
    grad_readout_ref[...] = pltpu.roll(total, shift, 1)[:, :own_size]
    for copy in copies:
        copy.wait()


def on_device(
    queries,
    key_heads,
    value_heads,
    upper_cotangent,
    readout,
    base_value,
    old_values,
    returns,
    source_index,
    doc_lengths,
):
    seq_count = lax.axis_size("seq")
    dp_count = lax.axis_size("dp")
    tok_dev, _ = queries.shape
    head_count, head_size = readout.shape
    kv_width = key_heads.shape[1]
    kv_count = kv_width // head_size
    per_group = head_count // kv_count
    wide = per_group * tok_dev
    own_heads, own_size = head_count // seq_count, head_size // dp_count
    longest = tok_dev * seq_count // 2
    back = min(seq_count - 1, (longest - 1 + tok_dev - 1) // tok_dev)
    span = (back + 1) * tok_dev
    relay = seq_count == 4 and back == 2

    def send(array, pairs, axis="seq"):
        return lax.ppermute(array, axis, pairs)

    def swap(array, bit, axis="seq"):
        return send(array, [(i, i ^ bit) for i in range(lax.axis_size(axis))], axis)

    def rotate(array, shift):
        return send(array, [(i, (i + shift) % seq_count) for i in range(seq_count)])

    vmem = pl.BlockSpec(memory_space=pltpu.VMEM)
    hbm = pl.BlockSpec(memory_space=pltpu.HBM)
    f32, bf16 = jnp.float32, jnp.bfloat16
    room = 8 + (kv_count * wide * span * 4 >> 20)
    unit = 2 * head_count * tok_dev * tok_dev * head_size

    def call(kernel, outs, args, megabytes=4, flops=1000, **more):
        more.setdefault("in_specs", [vmem] * len(args))
        more.setdefault("out_specs", [vmem] * len(outs))
        args = [
            pltpu.with_memory_space_constraint(arg, pltpu.HBM) if spec is hbm else arg
            for arg, spec in zip(args, more["in_specs"])
        ]
        return pl.pallas_call(
            kernel,
            out_shape=[jax.ShapeDtypeStruct(*out) for out in outs],
            compiler_params=pltpu.CompilerParams(vmem_limit_bytes=megabytes << 20),
            cost_estimate=pl.CostEstimate(
                flops=flops, bytes_accessed=flops // 1000, transcendentals=0
            ),
            **more,
        )(*args)

    def swap_rows(at):
        return [swap(array, at).reshape(1, tok_dev) for array in (old_values, returns)]

    small = ((1, tok_dev), f32)
    keys, vals = [], []
    if relay:
        key_far = swap(key_heads, 2)
        key_near = swap(key_heads, 1)
        pack, pair = call(
            pack_kernel,
            [((tok_dev + 16, kv_width), bf16), ((2, tok_dev), f32)],
            [value_heads, old_values.reshape(1, tok_dev), returns.reshape(1, tok_dev)],
            in_specs=[hbm] * 3,
            scratch_shapes=[pltpu.VMEM(*small), pltpu.VMEM(*small), pltpu.SemaphoreType.DMA((3,))],
        )
        value_far = rotate(pack, 2)
        value_ring = rotate(pack, 1)
        keys = [key_near, swap(key_far, 1), key_far]
        vals = [value_ring, value_far]
        row_args = [pack, value_ring, value_far, rotate(pair, 3)]
    else:
        seen = [swap_rows(at) for at in range(1, seq_count)]
        for step in range(1, back + 1):
            keys.append(rotate(key_heads, step))
            vals.append(rotate(value_heads, step))
    outs = call(
        functools.partial(own_kernel, back, kv_count),
        [
            (queries.shape, bf16),
            (key_heads.shape, bf16),
            (value_heads.shape, bf16),
            (upper_cotangent.shape, bf16),
            (readout.shape, bf16),
            small,
            (source_index.shape, jnp.int32),
            small,
            small,
            ((kv_count, head_size, wide), bf16),
            ((kv_count, tok_dev, wide), f32),
            ((kv_count, head_size, wide), f32),
            ((2, kv_count, wide), f32),
            ((back * tok_dev, tok_dev), f32),
        ],
        [
            doc_lengths,
            queries,
            key_heads,
            value_heads,
            upper_cotangent,
            readout,
            base_value.reshape(1, tok_dev),
            source_index,
            old_values.reshape(1, tok_dev),
            returns.reshape(1, tok_dev),
        ],
        room,
        2 * unit,
        in_specs=[hbm] * 10,
        scratch_shapes=[
            pltpu.SMEM(doc_lengths.shape, jnp.int32),
            pltpu.SemaphoreType.DMA((10,)),
        ],
    )
    query_here, key_here, value_here, upper_here, readout_here, base_here = outs[:6]
    source_here, old_here, return_here = outs[6:9]
    turned_query, own_raised, own_sum, own_stat, bias = outs[9:]
    if not relay:
        row_args = [old_here] + [rows[0] for rows in seen]
        row_args += [return_here] + [rows[1] for rows in seen]
    (now,) = call(
        functools.partial(source_kernel, seq_count, relay),
        [((2, tok_dev), f32)],
        [source_here, *row_args],
        8,
    )
    bit = seq_count // 2
    size = head_count // 2
    outs = call(
        functools.partial(forward_kernel, back, kv_count, relay, bit),
        [
            ((2, tok_dev), f32),
            ((kv_count, back * tok_dev, wide), f32),
            ((kv_count, head_size, wide), bf16),
            ((2, kv_count, wide), f32),
            (key_heads.shape, bf16),
            ((size, head_size), f32),
            ((size, head_size), f32),
        ],
        [bias, now, base_here, readout_here, turned_query, own_sum, own_stat] + keys + vals,
        room,
        2 * back * unit,
        scratch_shapes=[pltpu.VMEM((head_count, head_size), f32)],
    )
    rows, raised, out, norm, near, keep, away = outs
    keys = [near] + keys[1 + relay :]
    far = swap(away, bit)
    outs = call(
        functools.partial(backward_kernel, back, kv_count),
        [
            ((kv_count, wide), f32),
            ((kv_count, wide, head_size), bf16),
            ((kv_count, head_size, wide), bf16),
            ((kv_count, back * tok_dev, wide), bf16),
        ]
        + [((tok_dev, 2 * kv_width), bf16)] * back,
        [rows, upper_here, readout_here, raised, norm, out, query_here] + vals,
        room,
        3 * back * unit,
    )
    delta, cot, turned_cot, grad_scores = outs[:4]
    grads = outs[4:]
    while bit > 1:
        bit, size = bit // 2, size // 2
        keep, away = call(
            functools.partial(halve_kernel, bit),
            [((size, head_size), f32)] * 2,
            [keep, far],
            scratch_shapes=[pltpu.VMEM((2 * size, head_size), f32)],
        )
        far = swap(away, bit)
    returned = [rotate(grads[step - 1], -step) for step in range(1, back + 1)]

    def spread(left, right, bit):
        (total,) = call(sum_kernel, [((own_heads, head_size), f32)], [left, right])
        return total, swap(total, bit, "dp")

    def query_part(groups):
        args = [own_raised, norm, delta, cot, turned_cot, grad_scores, query_here, key_here]
        args += keys + [value_here]
        width = len(groups) * head_size
        return call(
            functools.partial(query_grad_kernel, back, kv_count, groups),
            [
                ((tok_dev, per_group * width), bf16),
                ((tok_dev, width), f32),
                ((tok_dev, width), f32),
            ],
            args,
            room,
            (4 + back) * unit * len(groups) // kv_count,
        )

    bits = [1 << at for at in range(dp_count.bit_length() - 1)]
    splits = [range(0, kv_count // 2), range(kv_count // 2, kv_count - 1)]
    splits += [range(kv_count - 1, kv_count)]
    pieces = []
    for at, bit in enumerate(bits):
        keep, far = spread(keep, far, bit)
        if at < len(splits):
            pieces += query_part(splits[at])
    for at in range(len(bits), len(splits)):
        pieces += query_part(splits[at])
    new_values, grad_queries, grad_key_heads, grad_value_heads, grad_readout = call(
        functools.partial(combine_kernel, len(splits)),
        [
            small,
            (queries.shape, bf16),
            (key_heads.shape, bf16),
            (key_heads.shape, bf16),
            ((own_heads, own_size), f32),
        ],
        pieces + [rows, keep, far] + returned,
        8,
        unit // 100,
        out_specs=[vmem, hbm, vmem, vmem, vmem],
        scratch_shapes=[pltpu.SemaphoreType.DMA((len(splits),))],
    )
    return (
        new_values.reshape(tok_dev),
        grad_queries,
        grad_key_heads,
        grad_value_heads,
        grad_readout,
    )


def solution(mesh):
    return jax.shard_map(
        on_device,
        mesh=mesh,
        in_specs=(
            P(("dp", "seq"), None),
            P(("dp", "seq"), None),
            P(("dp", "seq"), None),
            P(("dp", "seq"), None),
            P(),
            P(("dp", "seq")),
            P(("dp", "seq")),
            P(("dp", "seq")),
            P("dp", None),
            P("dp", None),
        ),
        out_specs=(
            P(("dp", "seq")),
            P(("dp", "seq"), None),
            P(("dp", "seq"), None),
            P(("dp", "seq"), None),
            P("seq", "dp"),
        ),
        check_vma=False,
    )
```

```python
import functools

import jax
import jax.numpy as jnp
from jax import lax
from jax.experimental import pallas as pl
from jax.experimental.pallas import tpu as pltpu
from jax.sharding import PartitionSpec as P


clip_range = 0.2
smooth_width = 0.1
loss_scale = 16.0


def value_grad(values, old_now, return_now):
    ratio = jnp.tanh((values - old_now) / clip_range)
    clipped = old_now + clip_range * ratio
    plain_gap = values - return_now
    clip_gap = clipped - return_now
    mixing = jax.nn.sigmoid((plain_gap * plain_gap - clip_gap * clip_gap) / smooth_width)
    return loss_scale * (mixing * plain_gap + (1.0 - mixing) * clip_gap * (1.0 - ratio * ratio))


def dot(left, right, left_dim, right_dim):
    return lax.dot_general(
        left,
        right,
        (((left_dim,), (right_dim,)), ((), ())),
        preferred_element_type=jnp.float32,
    )


def block_bias(doc_ref, rank, tok_dev, key_block, blocks):
    shape = (blocks * tok_dev, tok_dev)
    keys = lax.broadcasted_iota(jnp.int32, shape, 0) + key_block * tok_dev
    places = lax.broadcasted_iota(jnp.int32, shape, 1) + rank * tok_dev
    first = jnp.zeros(shape, jnp.int32)
    start = 0
    for doc in range(doc_ref.shape[1] - 1):
        size = doc_ref[0, doc]
        start = start + size
        first = first + jnp.where(places >= start, size, 0)
    return jnp.where((keys <= places) & (keys >= first), 0.0, -1e30).astype(jnp.float32)


def diagonal_of(size):
    shape = (size, size)
    return lax.broadcasted_iota(jnp.int32, shape, 0) == lax.broadcasted_iota(jnp.int32, shape, 1)


def as_column(row, diagonal):
    return jnp.sum(jnp.where(diagonal, row, jnp.zeros_like(row)), axis=1, keepdims=True)


def lanes_of(group, size):
    return slice(group * size, (group + 1) * size)


def group_rows(refs, group, size):
    return jnp.concatenate([ref[:, lanes_of(group, size)] for ref in reversed(refs)], axis=0)


def stacked(ref, group, per_group, size):
    heads = range(group * per_group, (group + 1) * per_group)
    return jnp.concatenate([ref[:, lanes_of(h, size)] for h in heads], axis=0)


def thirds(array):
    high = array.astype(jnp.bfloat16).astype(jnp.float32)
    middle = (array - high).astype(jnp.bfloat16).astype(jnp.float32)
    return high, middle, array - high - middle


def load_kernel(back, *refs):
    hbm, outs, (doc_ref, old_ref, return_ref, sems) = refs[:9], refs[9:18], refs[18:]
    query_ref, key_ref, pack_ref, pair_ref, readout_ref, base_ref, source_ref = outs[:7]
    own_bias_ref, bias_ref = outs[7:]
    tok_dev = old_ref.shape[1]
    rank = lax.axis_index("seq")
    targets = (doc_ref, old_ref, return_ref, pack_ref.at[0:tok_dev, :], query_ref, key_ref)
    targets += (readout_ref, base_ref, source_ref)
    copies = [
        pltpu.make_async_copy(source, target, sems.at[at])
        for at, (source, target) in enumerate(zip(hbm, targets))
    ]
    for copy in copies:
        copy.start()
    for copy in copies[:3]:
        copy.wait()
    own_bias_ref[...] = block_bias(doc_ref, rank, tok_dev, rank, 1)
    bias_ref[...] = block_bias(doc_ref, rank, tok_dev, rank - back, back)
    places = lax.broadcasted_iota(jnp.int32, (16, tok_dev), 0)
    tile = jnp.zeros((16, tok_dev), jnp.float32)
    for at, third in enumerate(thirds(old_ref[...]) + thirds(return_ref[...])):
        tile = jnp.where(places == at, third, tile)
    pair_ref[0:1, :] = old_ref[...]
    pair_ref[1:2, :] = return_ref[...]
    pack_ref[tok_dev:, :] = jnp.zeros((16, pack_ref.shape[1]), jnp.bfloat16)
    pack_ref[tok_dev:, 0:tok_dev] = tile.astype(jnp.bfloat16)
    for copy in copies[3:]:
        copy.wait()


def own_kernel(kv_count, query_ref, key_ref, pack_ref, bias_ref, *refs):
    qt_ref, raised_ref, sum_ref, stat_ref = refs
    tok_dev, head_size = query_ref.shape[0], key_ref.shape[1] // kv_count
    per_group = query_ref.shape[1] // head_size // kv_count
    scale = head_size**-0.5
    bias = jnp.tile(bias_ref[...], (1, per_group))
    for group in range(kv_count):
        for at in range(per_group):
            tile = query_ref[:, lanes_of(group * per_group + at, head_size)]
            qt_ref[group, :, lanes_of(at, tok_dev)] = tile.T
        scores = dot(key_ref[:, lanes_of(group, head_size)], qt_ref[group], 1, 0)
        scores = scores * scale + bias
        top = jnp.max(scores, axis=0, keepdims=True)
        raised = jnp.exp(scores - top)
        raised_ref[group] = raised
        stat_ref[0, group : group + 1, :] = top
        stat_ref[1, group : group + 1, :] = jnp.sum(raised, axis=0, keepdims=True)
        values = pack_ref[0:tok_dev, lanes_of(group, head_size)]
        sum_ref[group] = dot(values, raised.astype(jnp.bfloat16), 0, 0)


def upper_kernel(upper_hbm, upper_ref, sem):
    copy = pltpu.make_async_copy(upper_hbm, upper_ref, sem)
    copy.start()
    copy.wait()


def source_kernel(seq_count, source_ref, *refs):
    row_refs, out_ref = refs[:-1], refs[-1]
    tok_dev = out_ref.shape[1]
    rank = lax.axis_index("seq")
    diagonal = diagonal_of(tok_dev)
    places = lax.broadcasted_iota(jnp.int32, (tok_dev, tok_dev), 0)
    own = source_ref[:, pl.ds(pl.multiple_of(rank * tok_dev, tok_dev), tok_dev)]
    found = [jnp.zeros((1, tok_dev), jnp.float32)] * 2
    for at in range(seq_count):
        owner = lax.rem(rank - at + seq_count, seq_count)
        chosen = places + owner * tok_dev == own
        for kind in range(2):
            if row_refs[at].shape[0] > 2:
                tile = row_refs[at][tok_dev:, 0:tok_dev].astype(jnp.float32)
                row = tile[3 * kind : 3 * kind + 1] + tile[3 * kind + 1 : 3 * kind + 2]
                row = row + tile[3 * kind + 2 : 3 * kind + 3]
            else:
                row = row_refs[at][kind : kind + 1, :]
            column = as_column(row, diagonal)
            found[kind] = found[kind] + jnp.sum(
                jnp.where(chosen, column, 0.0), axis=0, keepdims=True
            )
    for kind in range(2):
        out_ref[kind : kind + 1, :] = found[kind]


def readout_terms(row, out_ref, whole_ref):
    kv_count, _, wide = out_ref.shape
    tok_dev = row.shape[1]
    per_group = wide // tok_dev
    high, middle, low = thirds(row)
    places = lax.broadcasted_iota(jnp.int32, (16, tok_dev), 0)
    rows = jnp.where(
        places == 0, high, jnp.where(places == 1, middle, jnp.where(places == 2, low, 0.0))
    ).astype(jnp.bfloat16)
    for group in range(kv_count):
        for at in range(per_group):
            h = group * per_group + at
            terms = dot(rows, out_ref[group, :, lanes_of(at, tok_dev)], 1, 1)
            whole_ref[h : h + 1, :] = jnp.sum(terms, axis=0, keepdims=True)


def forward_kernel(back, kv_count, relay, bit, *refs):
    bias_ref, now_ref, base_ref, readout_ref, qt_ref, sum_ref, stat_ref = refs[:7]
    key_refs, value_refs = refs[7 : 7 + back + relay], refs[7 + back + relay : 7 + 2 * back + relay]
    refs = refs[7 + 2 * back + relay :]
    rows_ref, raised_ref, out_ref, norm_ref, near_ref, keep_ref, send_ref, whole_ref = refs
    tok_dev = bias_ref.shape[1]
    head_count, head_size = readout_ref.shape
    per_group = head_count // kv_count
    scale = head_size**-0.5
    near_ref[...] = key_refs[0][...]
    if relay:
        near_ref[...] = jnp.where(
            lax.axis_index("seq") % 2 == 1, key_refs[0][...], key_refs[1][...]
        )
    key_refs = (near_ref,) + tuple(key_refs[1 + relay :])
    value_refs = [ref.at[0:tok_dev, :] for ref in value_refs]
    bias = jnp.tile(bias_ref[...], (1, per_group))
    total = base_ref[...]
    for group in range(kv_count):
        scores = dot(group_rows(key_refs, group, head_size), qt_ref[group], 1, 0)
        scores = scores * scale + bias
        own_top = stat_ref[0, group : group + 1, :]
        top = jnp.maximum(jnp.max(scores, axis=0, keepdims=True), own_top)
        raised = jnp.exp(scores - top)
        raised_ref[group] = raised
        shrink = jnp.exp(own_top - top)
        inverse = 1.0 / (
            jnp.sum(raised, axis=0, keepdims=True) + shrink * stat_ref[1, group : group + 1, :]
        )
        norm_ref[0, group : group + 1, :] = inverse
        norm_ref[1, group : group + 1, :] = shrink * inverse
        out = dot(group_rows(value_refs, group, head_size), raised.astype(jnp.bfloat16), 0, 0)
        out = ((out + sum_ref[group] * shrink) * inverse).astype(jnp.bfloat16)
        out_ref[group] = out
        terms = dot(readout_ref[group * per_group : (group + 1) * per_group, :], out, 1, 0)
        for at in range(per_group):
            total = total + terms[at : at + 1, lanes_of(at, tok_dev)]
    value_cot = value_grad(total, now_ref[0:1, :], now_ref[1:2, :])
    rows_ref[0:1, :] = total
    rows_ref[1:2, :] = value_cot
    readout_terms(value_cot, out_ref, whole_ref)
    halve(whole_ref, bit, keep_ref, send_ref)


def backward_kernel(back, kv_count, *refs):
    rows_ref, upper_ref, readout_ref, raised_ref, norm_ref, out_ref, query_ref = refs[:7]
    tok_dev = query_ref.shape[0]
    value_refs = [ref.at[0:tok_dev, :] for ref in refs[7 : 7 + back]]
    delta_ref, cot_ref, ct_ref, grad_score_ref = refs[7 + back : 11 + back]
    grad_refs = refs[11 + back :]
    head_count, head_size = readout_ref.shape
    per_group = head_count // kv_count
    scale = head_size**-0.5
    value_cot = rows_ref[1:2, :]
    column = jnp.broadcast_to(as_column(value_cot, diagonal_of(tok_dev)), (tok_dev, head_size))
    for group in range(kv_count):
        cots = []
        for at in range(per_group):
            h = group * per_group + at
            cot = (
                upper_ref[:, lanes_of(h, head_size)].astype(jnp.float32)
                + column * readout_ref[h : h + 1, :].astype(jnp.float32)
            ).astype(jnp.bfloat16)
            cots.append(cot)
            ct_ref[group, :, lanes_of(at, tok_dev)] = cot.T
        cot = jnp.concatenate(cots, axis=0)
        cot_ref[group] = cot
        turned = ct_ref[group]
        delta = jnp.sum(
            turned.astype(jnp.float32) * out_ref[group].astype(jnp.float32), axis=0, keepdims=True
        )
        delta_ref[group : group + 1, :] = delta
        weights = raised_ref[group] * norm_ref[0, group : group + 1, :]
        grad_value = dot(weights.astype(jnp.bfloat16), cot, 1, 0).astype(jnp.bfloat16)
        grad_weights = dot(group_rows(value_refs, group, head_size), turned, 1, 0)
        grad_scores = (weights * ((grad_weights - delta) * scale)).astype(jnp.bfloat16)
        grad_score_ref[group] = grad_scores
        grad_key = dot(grad_scores, stacked(query_ref, group, per_group, head_size), 1, 0)
        grad_key = grad_key.astype(jnp.bfloat16)
        for step in range(1, back + 1):
            block = slice((back - step) * tok_dev, (back - step + 1) * tok_dev)
            grad_refs[step - 1][:, lanes_of(group, head_size)] = grad_key[block]
            grad_refs[step - 1][:, lanes_of(kv_count + group, head_size)] = grad_value[block]


def halve(whole_ref, bit, keep_ref, send_ref):
    rows = keep_ref.shape[0]
    mine = lax.rem(lax.div(lax.axis_index("seq"), bit), 2)
    keep_ref[...] = whole_ref[pl.ds(pl.multiple_of(mine * rows, rows), rows), :]
    send_ref[...] = whole_ref[pl.ds(pl.multiple_of((1 - mine) * rows, rows), rows), :]


def halve_kernel(bit, left_ref, right_ref, keep_ref, send_ref, whole_ref):
    whole_ref[...] = left_ref[...] + right_ref[...]
    halve(whole_ref, bit, keep_ref, send_ref)


def sum_kernel(left_ref, right_ref, out_ref):
    out_ref[...] = left_ref[...] + right_ref[...]


def query_grad_kernel(back, kv_count, groups, *refs):
    raised_ref, norm_ref, delta_ref, cot_ref, ct_ref, score_ref, query_ref = refs[:7]
    key_refs, pack_ref = refs[7 : 8 + back], refs[8 + back]
    grad_query_ref, own_key_ref, own_value_ref, piece_ref, sems = refs[-5:]
    tok_dev = query_ref.shape[0]
    head_size = ct_ref.shape[1]
    per_group = query_ref.shape[1] // head_size // kv_count
    scale = head_size**-0.5
    copies = []
    for at_group, group in enumerate(groups):
        lanes, own_lanes = lanes_of(group, head_size), lanes_of(at_group, head_size)
        grad_weights = dot(pack_ref[0:tok_dev, lanes], ct_ref[group], 1, 0)
        weights = raised_ref[group] * norm_ref[1, group : group + 1, :]
        grad_scores = weights * ((grad_weights - delta_ref[group : group + 1, :]) * scale)
        grad_scores = grad_scores.astype(jnp.bfloat16)
        scores = jnp.concatenate([score_ref[group], grad_scores], axis=0)
        grad_query = dot(group_rows(key_refs, group, head_size), scores, 0, 0)
        for at in range(per_group):
            turned = grad_query[:, lanes_of(at, tok_dev)].T
            piece_ref[at_group, :, lanes_of(at, head_size)] = turned.astype(jnp.bfloat16)
        wide = lanes_of(group, per_group * head_size)
        copies.append(
            pltpu.make_async_copy(
                piece_ref.at[at_group], grad_query_ref.at[:, wide], sems.at[at_group]
            )
        )
        copies[-1].start()
        own_key_ref[:, own_lanes] = dot(
            grad_scores, stacked(query_ref, group, per_group, head_size), 1, 0
        )
        own_value_ref[:, own_lanes] = dot(weights.astype(jnp.bfloat16), cot_ref[group], 1, 0)
    for copy in copies:
        copy.wait()


def combine_kernel(sections, *refs):
    own_refs, refs = refs[: 2 * sections], refs[2 * sections :]
    rows_ref, left_ref, right_ref = refs[:3]
    back_refs = refs[3:-4]
    values_ref, grad_key_ref, grad_value_ref, grad_readout_ref = refs[-4:]
    values_ref[...] = rows_ref[0:1, :]
    for kind, out_ref in ((0, grad_key_ref), (1, grad_value_ref)):
        left = 0
        for section in range(sections):
            total = own_refs[2 * section + kind][...]
            right = left + total.shape[1]
            start = kind * out_ref.shape[1]
            for other in back_refs:
                total = total + other[:, start + left : start + right].astype(jnp.float32)
            out_ref[:, left:right] = total.astype(jnp.bfloat16)
            left = right
    total = left_ref[...] + right_ref[...]
    wide, own_size = total.shape[1], grad_readout_ref.shape[1]
    shift = lax.rem(wide - lax.axis_index("dp") * own_size, wide)
    grad_readout_ref[...] = pltpu.roll(total, shift, 1)[:, :own_size]


def on_device(
    queries,
    key_heads,
    value_heads,
    upper_cotangent,
    readout,
    base_value,
    old_values,
    returns,
    source_index,
    doc_lengths,
):
    seq_count = lax.axis_size("seq")
    dp_count = lax.axis_size("dp")
    tok_dev, _ = queries.shape
    head_count, head_size = readout.shape
    kv_width = key_heads.shape[1]
    kv_count = kv_width // head_size
    per_group = head_count // kv_count
    wide = per_group * tok_dev
    own_heads, own_size = head_count // seq_count, head_size // dp_count
    longest = tok_dev * seq_count // 2
    back = min(seq_count - 1, (longest - 1 + tok_dev - 1) // tok_dev)
    span = (back + 1) * tok_dev
    relay = seq_count == 4 and back == 2

    def send(array, pairs, axis="seq"):
        return lax.ppermute(array, axis, pairs)

    def swap(array, bit, axis="seq"):
        return send(array, [(i, i ^ bit) for i in range(lax.axis_size(axis))], axis)

    def rotate(array, shift):
        return send(array, [(i, (i + shift) % seq_count) for i in range(seq_count)])

    vmem = pl.BlockSpec(memory_space=pltpu.VMEM)
    hbm = pl.BlockSpec(memory_space=pltpu.HBM)
    f32, bf16 = jnp.float32, jnp.bfloat16
    room = 8 + (kv_count * wide * span * 4 >> 20)
    unit = 2 * head_count * tok_dev * tok_dev * head_size

    def call(kernel, outs, args, megabytes=4, flops=1000, **more):
        more.setdefault("in_specs", [vmem] * len(args))
        more.setdefault("out_specs", [vmem] * len(outs))
        args = [
            pltpu.with_memory_space_constraint(arg, pltpu.HBM) if spec is hbm else arg
            for arg, spec in zip(args, more["in_specs"])
        ]
        return pl.pallas_call(
            kernel,
            out_shape=[jax.ShapeDtypeStruct(*out) for out in outs],
            compiler_params=pltpu.CompilerParams(vmem_limit_bytes=megabytes << 20),
            cost_estimate=pl.CostEstimate(
                flops=flops, bytes_accessed=flops // 1000, transcendentals=0
            ),
            **more,
        )(*args)

    small = ((1, tok_dev), f32)
    if relay:
        key_far = swap(key_heads, 2)
    outs = call(
        functools.partial(load_kernel, back),
        [
            (queries.shape, bf16),
            (key_heads.shape, bf16),
            ((tok_dev + 16, kv_width), bf16),
            ((2, tok_dev), f32),
            (readout.shape, bf16),
            small,
            (source_index.shape, jnp.int32),
            ((tok_dev, tok_dev), f32),
            ((back * tok_dev, tok_dev), f32),
        ],
        [
            doc_lengths,
            old_values.reshape(1, tok_dev),
            returns.reshape(1, tok_dev),
            value_heads,
            queries,
            key_heads,
            readout,
            base_value.reshape(1, tok_dev),
            source_index,
        ],
        8,
        in_specs=[hbm] * 9,
        scratch_shapes=[
            pltpu.SMEM(doc_lengths.shape, jnp.int32),
            pltpu.VMEM(*small),
            pltpu.VMEM(*small),
            pltpu.SemaphoreType.DMA((9,)),
        ],
    )
    query_here, key_here, pack, pair, readout_here, base_here, source_here, own_bias, bias = outs
    if relay:
        value_far = rotate(pack, 2)
        value_ring = rotate(pack, 1)
        key_near = swap(key_heads, 1)
        keys = [key_near, swap(key_far, 1), key_far]
        row_args = [pair, value_ring, value_far, rotate(pair, 3)]
        vals = [value_ring, value_far]
    else:
        row_args = [pair] + [rotate(pair, at) for at in range(1, seq_count)]
        keys, vals = [], []
        for step in range(1, back + 1):
            keys.append(rotate(key_heads, step))
            vals.append(rotate(value_heads, step))
    turned_query, own_raised, own_sum, own_stat = call(
        functools.partial(own_kernel, kv_count),
        [
            ((kv_count, head_size, wide), bf16),
            ((kv_count, tok_dev, wide), f32),
            ((kv_count, head_size, wide), f32),
            ((2, kv_count, wide), f32),
        ],
        [query_here, key_here, pack, own_bias],
        room,
        2 * unit,
    )
    (upper_here,) = call(
        upper_kernel,
        [(upper_cotangent.shape, bf16)],
        [upper_cotangent],
        in_specs=[hbm],
        scratch_shapes=[pltpu.SemaphoreType.DMA],
    )
    (now,) = call(
        functools.partial(source_kernel, seq_count),
        [((2, tok_dev), f32)],
        [source_here, *row_args],
        8,
    )
    bit = seq_count // 2
    size = head_count // 2
    args = [bias, now, base_here, readout_here, turned_query, own_sum, own_stat]
    args += keys + vals
    outs = call(
        functools.partial(forward_kernel, back, kv_count, relay, bit),
        [
            ((2, tok_dev), f32),
            ((kv_count, back * tok_dev, wide), f32),
            ((kv_count, head_size, wide), bf16),
            ((2, kv_count, wide), f32),
            (key_heads.shape, bf16),
            ((size, head_size), f32),
            ((size, head_size), f32),
        ],
        args,
        room,
        2 * back * unit,
        scratch_shapes=[pltpu.VMEM((head_count, head_size), f32)],
    )
    rows, raised, out, norm, near, keep, away = outs
    keys = [near] + keys[1 + relay :]
    far = swap(away, bit)
    delta, cot, turned_cot, grad_scores, *grads = call(
        functools.partial(backward_kernel, back, kv_count),
        [
            ((kv_count, wide), f32),
            ((kv_count, wide, head_size), bf16),
            ((kv_count, head_size, wide), bf16),
            ((kv_count, back * tok_dev, wide), bf16),
        ]
        + [((tok_dev, 2 * kv_width), bf16)] * back,
        [rows, upper_here, readout_here, raised, norm, out, query_here] + vals,
        room,
        3 * back * unit,
    )
    while bit > 1:
        bit, size = bit // 2, size // 2
        keep, away = call(
            functools.partial(halve_kernel, bit),
            [((size, head_size), f32)] * 2,
            [keep, far],
            scratch_shapes=[pltpu.VMEM((2 * size, head_size), f32)],
        )
        far = swap(away, bit)
    returned = [rotate(grads[step - 1], -step) for step in range(1, back + 1)]

    def spread(left, right, bit):
        (total,) = call(sum_kernel, [((own_heads, head_size), f32)], [left, right])
        return total, swap(total, bit, "dp")

    def query_part(groups, base):
        args = [own_raised, norm, delta, cot, turned_cot, grad_scores, query_here, key_here]
        args += keys + [pack]
        aliases = {} if base is None else {len(args): 0}
        specs = [vmem] * len(args) + [hbm] * len(aliases)
        args += [] if base is None else [base]
        width = len(groups) * head_size
        return call(
            functools.partial(query_grad_kernel, back, kv_count, groups),
            [(queries.shape, bf16), ((tok_dev, width), f32), ((tok_dev, width), f32)],
            args,
            room,
            (4 + back) * unit * len(groups) // kv_count,
            in_specs=specs,
            out_specs=[hbm, vmem, vmem],
            scratch_shapes=[
                pltpu.VMEM((len(groups), tok_dev, per_group * head_size), bf16),
                pltpu.SemaphoreType.DMA((len(groups),)),
            ],
            input_output_aliases=aliases,
        )

    half = max(1, kv_count - 1)
    splits = [range(0, 1), range(1, half), range(half, kv_count)]
    own_parts, grad_queries = [], None
    for at in range(dp_count.bit_length() - 1):
        keep, far = spread(keep, far, 1 << at)
        if at < len(splits):
            grad_queries, *parts = query_part(splits[at], grad_queries)
            own_parts += parts
    new_values, grad_key_heads, grad_value_heads, grad_readout = call(
        functools.partial(combine_kernel, len(splits)),
        [small, (key_heads.shape, bf16), (key_heads.shape, bf16), ((own_heads, own_size), f32)],
        own_parts + [rows, keep, far] + returned,
        8,
        unit // 100,
    )
    return (
        new_values.reshape(tok_dev),
        grad_queries,
        grad_key_heads,
        grad_value_heads,
        grad_readout,
    )


def solution(mesh):
    return jax.shard_map(
        on_device,
        mesh=mesh,
        in_specs=(
            P(("dp", "seq"), None),
            P(("dp", "seq"), None),
            P(("dp", "seq"), None),
            P(("dp", "seq"), None),
            P(),
            P(("dp", "seq")),
            P(("dp", "seq")),
            P(("dp", "seq")),
            P("dp", None),
            P("dp", None),
        ),
        out_specs=(
            P(("dp", "seq")),
            P(("dp", "seq"), None),
            P(("dp", "seq"), None),
            P(("dp", "seq"), None),
            P("seq", "dp"),
        ),
        check_vma=False,
    )
```

```python
import functools

import jax
import jax.numpy as jnp
from jax import lax
from jax.experimental import pallas as pl
from jax.experimental.pallas import tpu as pltpu
from jax.sharding import PartitionSpec as P


clip_range = 0.2
smooth_width = 0.1
loss_scale = 16.0


def value_grad(values, old_now, return_now):
    ratio = jnp.tanh((values - old_now) / clip_range)
    clipped = old_now + clip_range * ratio
    plain_gap = values - return_now
    clip_gap = clipped - return_now
    mixing = jax.nn.sigmoid((plain_gap * plain_gap - clip_gap * clip_gap) / smooth_width)
    return loss_scale * (mixing * plain_gap + (1.0 - mixing) * clip_gap * (1.0 - ratio * ratio))


def dot(left, right, left_dim, right_dim):
    return lax.dot_general(
        left,
        right,
        (((left_dim,), (right_dim,)), ((), ())),
        preferred_element_type=jnp.float32,
    )


def block_bias(doc_ref, rank, tok_dev, key_block, blocks):
    shape = (blocks * tok_dev, tok_dev)
    keys = lax.broadcasted_iota(jnp.int32, shape, 0) + key_block * tok_dev
    places = lax.broadcasted_iota(jnp.int32, shape, 1) + rank * tok_dev
    first = jnp.zeros(shape, jnp.int32)
    start = 0
    for doc in range(doc_ref.shape[1] - 1):
        size = doc_ref[0, doc]
        start = start + size
        first = first + jnp.where(places >= start, size, 0)
    return jnp.where((keys <= places) & (keys >= first), 0.0, -1e30).astype(jnp.float32)


def diagonal_of(size):
    shape = (size, size)
    return lax.broadcasted_iota(jnp.int32, shape, 0) == lax.broadcasted_iota(jnp.int32, shape, 1)


def as_column(row, diagonal):
    return jnp.sum(jnp.where(diagonal, row, jnp.zeros_like(row)), axis=1, keepdims=True)


def lanes_of(group, size):
    return slice(group * size, (group + 1) * size)


def group_rows(refs, group, size):
    return jnp.concatenate([ref[:, lanes_of(group, size)] for ref in reversed(refs)], axis=0)


def stacked(ref, group, per_group, size):
    heads = range(group * per_group, (group + 1) * per_group)
    return jnp.concatenate([ref[:, lanes_of(h, size)] for h in heads], axis=0)


def thirds(array):
    high = array.astype(jnp.bfloat16).astype(jnp.float32)
    middle = (array - high).astype(jnp.bfloat16).astype(jnp.float32)
    return high, middle, array - high - middle


def pack_kernel(value_hbm, old_hbm, return_hbm, pack_ref, pair_ref, old_ref, return_ref, sems):
    tok_dev = old_ref.shape[1]
    copies = [
        pltpu.make_async_copy(old_hbm, old_ref, sems.at[0]),
        pltpu.make_async_copy(return_hbm, return_ref, sems.at[1]),
        pltpu.make_async_copy(value_hbm, pack_ref.at[0:tok_dev, :], sems.at[2]),
    ]
    for copy in copies:
        copy.start()
    for copy in copies[:2]:
        copy.wait()
    places = lax.broadcasted_iota(jnp.int32, (16, tok_dev), 0)
    tile = jnp.zeros((16, tok_dev), jnp.float32)
    for at, third in enumerate(thirds(old_ref[...]) + thirds(return_ref[...])):
        tile = jnp.where(places == at, third, tile)
    pair_ref[0:1, :] = old_ref[...]
    pair_ref[1:2, :] = return_ref[...]
    pack_ref[tok_dev:, :] = jnp.zeros((16, pack_ref.shape[1]), jnp.bfloat16)
    pack_ref[tok_dev:, 0:tok_dev] = tile.astype(jnp.bfloat16)
    copies[2].wait()


def own_kernel(back, kv_count, *refs):
    hbm, targets, refs = refs[:10], refs[10:19], refs[19:]
    query_ref, key_ref, value_ref = targets[:3]
    qt_ref, raised_ref, sum_ref, stat_ref, bias_ref, doc_ref, sems = refs
    targets = (doc_ref,) + tuple(targets)
    tok_dev, head_size = query_ref.shape[0], key_ref.shape[1] // kv_count
    per_group = query_ref.shape[1] // head_size // kv_count
    rank = lax.axis_index("seq")
    scale = head_size**-0.5
    copies = [
        pltpu.make_async_copy(source, target, sems.at[at])
        for at, (source, target) in enumerate(zip(hbm, targets))
    ]
    for copy in copies:
        copy.start()
    copies[0].wait()
    bias_ref[...] = block_bias(doc_ref, rank, tok_dev, rank - back, back)
    bias = jnp.tile(block_bias(doc_ref, rank, tok_dev, rank, 1), (1, per_group))
    for copy in copies[1:4]:
        copy.wait()
    for group in range(kv_count):
        for at in range(per_group):
            tile = query_ref[:, lanes_of(group * per_group + at, head_size)]
            qt_ref[group, :, lanes_of(at, tok_dev)] = tile.T
        scores = dot(key_ref[:, lanes_of(group, head_size)], qt_ref[group], 1, 0)
        scores = scores * scale + bias
        top = jnp.max(scores, axis=0, keepdims=True)
        raised = jnp.exp(scores - top)
        raised_ref[group] = raised
        stat_ref[0, group : group + 1, :] = top
        stat_ref[1, group : group + 1, :] = jnp.sum(raised, axis=0, keepdims=True)
        sum_ref[group] = dot(
            value_ref[:, lanes_of(group, head_size)], raised.astype(jnp.bfloat16), 0, 0
        )
    for copy in copies[4:]:
        copy.wait()


def source_kernel(seq_count, relay, source_ref, *refs):
    row_refs, out_ref = refs[:-1], refs[-1]
    tok_dev = out_ref.shape[1]
    rank = lax.axis_index("seq")
    diagonal = diagonal_of(tok_dev)
    places = lax.broadcasted_iota(jnp.int32, (tok_dev, tok_dev), 0)
    own = source_ref[:, pl.ds(pl.multiple_of(rank * tok_dev, tok_dev), tok_dev)]
    found = [jnp.zeros((1, tok_dev), jnp.float32)] * 2
    for at in range(seq_count):
        owner = lax.rem(rank - at + seq_count, seq_count) if relay else rank ^ at
        chosen = places + owner * tok_dev == own
        for kind in range(2):
            if relay and at < seq_count - 1:
                tile = row_refs[at][tok_dev:, 0:tok_dev].astype(jnp.float32)
                row = tile[3 * kind : 3 * kind + 1] + tile[3 * kind + 1 : 3 * kind + 2]
                row = row + tile[3 * kind + 2 : 3 * kind + 3]
            elif relay:
                row = row_refs[at][kind : kind + 1, :]
            else:
                row = row_refs[kind * seq_count + at][...]
            column = as_column(row, diagonal)
            found[kind] = found[kind] + jnp.sum(
                jnp.where(chosen, column, 0.0), axis=0, keepdims=True
            )
    for kind in range(2):
        out_ref[kind : kind + 1, :] = found[kind]


def readout_terms(row, out_ref, whole_ref):
    kv_count, _, wide = out_ref.shape
    tok_dev = row.shape[1]
    per_group = wide // tok_dev
    high, middle, low = thirds(row)
    places = lax.broadcasted_iota(jnp.int32, (16, tok_dev), 0)
    rows = jnp.where(
        places == 0, high, jnp.where(places == 1, middle, jnp.where(places == 2, low, 0.0))
    ).astype(jnp.bfloat16)
    for group in range(kv_count):
        for at in range(per_group):
            h = group * per_group + at
            terms = dot(rows, out_ref[group, :, lanes_of(at, tok_dev)], 1, 1)
            whole_ref[h : h + 1, :] = jnp.sum(terms, axis=0, keepdims=True)


def forward_kernel(back, kv_count, relay, bit, *refs):
    bias_ref, now_ref, base_ref, readout_ref, qt_ref, sum_ref, stat_ref = refs[:7]
    key_refs, value_refs = refs[7 : 7 + back + relay], refs[7 + back + relay : 7 + 2 * back + relay]
    refs = refs[7 + 2 * back + relay :]
    rows_ref, raised_ref, out_ref, norm_ref, near_ref, keep_ref, send_ref, whole_ref = refs
    tok_dev = bias_ref.shape[1]
    head_count, head_size = readout_ref.shape
    per_group = head_count // kv_count
    scale = head_size**-0.5
    near_ref[...] = key_refs[0][...]
    if relay:
        near_ref[...] = jnp.where(
            lax.axis_index("seq") % 2 == 1, key_refs[0][...], key_refs[1][...]
        )
    key_refs = (near_ref,) + tuple(key_refs[1 + relay :])
    value_refs = [ref.at[0:tok_dev, :] for ref in value_refs]
    bias = jnp.tile(bias_ref[...], (1, per_group))
    total = base_ref[...]
    for group in range(kv_count):
        scores = dot(group_rows(key_refs, group, head_size), qt_ref[group], 1, 0)
        scores = scores * scale + bias
        own_top = stat_ref[0, group : group + 1, :]
        top = jnp.maximum(jnp.max(scores, axis=0, keepdims=True), own_top)
        raised = jnp.exp(scores - top)
        raised_ref[group] = raised
        shrink = jnp.exp(own_top - top)
        inverse = 1.0 / (
            jnp.sum(raised, axis=0, keepdims=True) + shrink * stat_ref[1, group : group + 1, :]
        )
        norm_ref[0, group : group + 1, :] = inverse
        norm_ref[1, group : group + 1, :] = shrink * inverse
        out = dot(group_rows(value_refs, group, head_size), raised.astype(jnp.bfloat16), 0, 0)
        out = ((out + sum_ref[group] * shrink) * inverse).astype(jnp.bfloat16)
        out_ref[group] = out
        terms = dot(readout_ref[group * per_group : (group + 1) * per_group, :], out, 1, 0)
        for at in range(per_group):
            total = total + terms[at : at + 1, lanes_of(at, tok_dev)]
    value_cot = value_grad(total, now_ref[0:1, :], now_ref[1:2, :])
    rows_ref[0:1, :] = total
    rows_ref[1:2, :] = value_cot
    readout_terms(value_cot, out_ref, whole_ref)
    halve(whole_ref, bit, keep_ref, send_ref)


def backward_kernel(back, kv_count, groups, *refs):
    rows_ref, upper_ref, readout_ref, raised_ref, norm_ref, out_ref, query_ref = refs[:7]
    tok_dev = query_ref.shape[0]
    value_refs = [ref.at[0:tok_dev, :] for ref in refs[7 : 7 + back]]
    earlier = refs[7 + back : -4 - back]
    delta_ref, cot_ref, ct_ref, grad_score_ref = refs[-4 - back : -back]
    grad_refs = refs[-back:]
    count = len(groups) if not earlier else kv_count
    head_count, head_size = readout_ref.shape
    per_group = head_count // kv_count
    scale = head_size**-0.5
    value_cot = rows_ref[1:2, :]
    column = jnp.broadcast_to(as_column(value_cot, diagonal_of(tok_dev)), (tok_dev, head_size))
    for local, group in enumerate(groups):
        cots = []
        for at in range(per_group):
            h = group * per_group + at
            cot = (
                upper_ref[:, lanes_of(h, head_size)].astype(jnp.float32)
                + column * readout_ref[h : h + 1, :].astype(jnp.float32)
            ).astype(jnp.bfloat16)
            cots.append(cot)
            ct_ref[local, :, lanes_of(at, tok_dev)] = cot.T
        cot = jnp.concatenate(cots, axis=0)
        cot_ref[local] = cot
        turned = ct_ref[local]
        delta = jnp.sum(
            turned.astype(jnp.float32) * out_ref[group].astype(jnp.float32), axis=0, keepdims=True
        )
        delta_ref[local : local + 1, :] = delta
        weights = raised_ref[group] * norm_ref[0, group : group + 1, :]
        grad_value = dot(weights.astype(jnp.bfloat16), cot, 1, 0).astype(jnp.bfloat16)
        grad_weights = dot(group_rows(value_refs, group, head_size), turned, 1, 0)
        grad_scores = (weights * ((grad_weights - delta) * scale)).astype(jnp.bfloat16)
        grad_score_ref[local] = grad_scores
        grad_key = dot(grad_scores, stacked(query_ref, group, per_group, head_size), 1, 0)
        grad_key = grad_key.astype(jnp.bfloat16)
        for step in range(1, back + 1):
            block = slice((back - step) * tok_dev, (back - step + 1) * tok_dev)
            place = group if earlier else local
            grad_refs[step - 1][:, lanes_of(place, head_size)] = grad_key[block]
            grad_refs[step - 1][:, lanes_of(count + place, head_size)] = grad_value[block]
    for step, piece_ref in enumerate(earlier):
        half = piece_ref.shape[1] // 2
        start = kv_count * head_size
        grad_refs[step][:, 0:half] = piece_ref[:, 0:half]
        grad_refs[step][:, start : start + half] = piece_ref[:, half:]


def halve(whole_ref, bit, keep_ref, send_ref):
    rows = keep_ref.shape[0]
    mine = lax.rem(lax.div(lax.axis_index("seq"), bit), 2)
    keep_ref[...] = whole_ref[pl.ds(pl.multiple_of(mine * rows, rows), rows), :]
    send_ref[...] = whole_ref[pl.ds(pl.multiple_of((1 - mine) * rows, rows), rows), :]


def halve_kernel(bit, left_ref, right_ref, keep_ref, send_ref, whole_ref):
    whole_ref[...] = left_ref[...] + right_ref[...]
    halve(whole_ref, bit, keep_ref, send_ref)


def sum_kernel(left_ref, right_ref, out_ref):
    out_ref[...] = left_ref[...] + right_ref[...]


def query_grad_kernel(back, kv_count, groups, *refs):
    raised_ref, norm_ref, delta_ref, cot_ref, ct_ref, score_ref, query_ref = refs[:7]
    key_refs, pack_ref = refs[7 : 8 + back], refs[8 + back]
    grad_query_ref, own_key_ref, own_value_ref, piece_ref, sems = refs[-5:]
    tok_dev = query_ref.shape[0]
    head_size = ct_ref.shape[1]
    per_group = query_ref.shape[1] // head_size // kv_count
    scale = head_size**-0.5
    copies = []
    for at_group, group in enumerate(groups):
        lanes, own_lanes = lanes_of(group, head_size), lanes_of(at_group, head_size)
        grad_weights = dot(pack_ref[0:tok_dev, lanes], ct_ref[at_group], 1, 0)
        weights = raised_ref[group] * norm_ref[1, group : group + 1, :]
        grad_scores = weights * ((grad_weights - delta_ref[at_group : at_group + 1, :]) * scale)
        grad_scores = grad_scores.astype(jnp.bfloat16)
        scores = jnp.concatenate([score_ref[at_group], grad_scores], axis=0)
        grad_query = dot(group_rows(key_refs, group, head_size), scores, 0, 0)
        for at in range(per_group):
            turned = grad_query[:, lanes_of(at, tok_dev)].T
            piece_ref[at_group, :, lanes_of(at, head_size)] = turned.astype(jnp.bfloat16)
        wide = lanes_of(group, per_group * head_size)
        copies.append(
            pltpu.make_async_copy(
                piece_ref.at[at_group], grad_query_ref.at[:, wide], sems.at[at_group]
            )
        )
        copies[-1].start()
        own_key_ref[:, own_lanes] = dot(
            grad_scores, stacked(query_ref, group, per_group, head_size), 1, 0
        )
        own_value_ref[:, own_lanes] = dot(weights.astype(jnp.bfloat16), cot_ref[at_group], 1, 0)
    for copy in copies:
        copy.wait()


def combine_kernel(sections, *refs):
    own_refs, refs = refs[: 2 * sections], refs[2 * sections :]
    rows_ref, left_ref, right_ref = refs[:3]
    back_refs = refs[3:-4]
    values_ref, grad_key_ref, grad_value_ref, grad_readout_ref = refs[-4:]
    values_ref[...] = rows_ref[0:1, :]
    for kind, out_ref in ((0, grad_key_ref), (1, grad_value_ref)):
        left = 0
        for section in range(sections):
            total = own_refs[2 * section + kind][...]
            right = left + total.shape[1]
            start = kind * out_ref.shape[1]
            for other in back_refs:
                total = total + other[:, start + left : start + right].astype(jnp.float32)
            out_ref[:, left:right] = total.astype(jnp.bfloat16)
            left = right
    total = left_ref[...] + right_ref[...]
    wide, own_size = total.shape[1], grad_readout_ref.shape[1]
    shift = lax.rem(wide - lax.axis_index("dp") * own_size, wide)
    grad_readout_ref[...] = pltpu.roll(total, shift, 1)[:, :own_size]


def on_device(
    queries,
    key_heads,
    value_heads,
    upper_cotangent,
    readout,
    base_value,
    old_values,
    returns,
    source_index,
    doc_lengths,
):
    seq_count = lax.axis_size("seq")
    dp_count = lax.axis_size("dp")
    tok_dev, _ = queries.shape
    head_count, head_size = readout.shape
    kv_width = key_heads.shape[1]
    kv_count = kv_width // head_size
    per_group = head_count // kv_count
    wide = per_group * tok_dev
    own_heads, own_size = head_count // seq_count, head_size // dp_count
    longest = tok_dev * seq_count // 2
    back = min(seq_count - 1, (longest - 1 + tok_dev - 1) // tok_dev)
    span = (back + 1) * tok_dev
    relay = seq_count == 4 and back == 2

    def send(array, pairs, axis="seq"):
        return lax.ppermute(array, axis, pairs)

    def swap(array, bit, axis="seq"):
        return send(array, [(i, i ^ bit) for i in range(lax.axis_size(axis))], axis)

    def rotate(array, shift):
        return send(array, [(i, (i + shift) % seq_count) for i in range(seq_count)])

    vmem = pl.BlockSpec(memory_space=pltpu.VMEM)
    hbm = pl.BlockSpec(memory_space=pltpu.HBM)
    f32, bf16 = jnp.float32, jnp.bfloat16
    room = 8 + (kv_count * wide * span * 4 >> 20)
    unit = 2 * head_count * tok_dev * tok_dev * head_size

    def call(kernel, outs, args, megabytes=4, flops=1000, **more):
        more.setdefault("in_specs", [vmem] * len(args))
        more.setdefault("out_specs", [vmem] * len(outs))
        args = [
            pltpu.with_memory_space_constraint(arg, pltpu.HBM) if spec is hbm else arg
            for arg, spec in zip(args, more["in_specs"])
        ]
        return pl.pallas_call(
            kernel,
            out_shape=[jax.ShapeDtypeStruct(*out) for out in outs],
            compiler_params=pltpu.CompilerParams(vmem_limit_bytes=megabytes << 20),
            cost_estimate=pl.CostEstimate(
                flops=flops, bytes_accessed=flops // 1000, transcendentals=0
            ),
            **more,
        )(*args)

    def swap_rows(at):
        return [swap(array, at).reshape(1, tok_dev) for array in (old_values, returns)]

    small = ((1, tok_dev), f32)
    keys, vals = [], []
    if relay:
        key_far = swap(key_heads, 2)
        key_near = swap(key_heads, 1)
        pack, pair = call(
            pack_kernel,
            [((tok_dev + 16, kv_width), bf16), ((2, tok_dev), f32)],
            [value_heads, old_values.reshape(1, tok_dev), returns.reshape(1, tok_dev)],
            in_specs=[hbm] * 3,
            scratch_shapes=[pltpu.VMEM(*small), pltpu.VMEM(*small), pltpu.SemaphoreType.DMA((3,))],
        )
        value_far = rotate(pack, 2)
        value_ring = rotate(pack, 1)
        keys = [key_near, swap(key_far, 1), key_far]
        vals = [value_ring, value_far]
        row_args = [pack, value_ring, value_far, rotate(pair, 3)]
    else:
        seen = [swap_rows(at) for at in range(1, seq_count)]
        for step in range(1, back + 1):
            keys.append(rotate(key_heads, step))
            vals.append(rotate(value_heads, step))
    outs = call(
        functools.partial(own_kernel, back, kv_count),
        [
            (queries.shape, bf16),
            (key_heads.shape, bf16),
            (value_heads.shape, bf16),
            (upper_cotangent.shape, bf16),
            (readout.shape, bf16),
            small,
            (source_index.shape, jnp.int32),
            small,
            small,
            ((kv_count, head_size, wide), bf16),
            ((kv_count, tok_dev, wide), f32),
            ((kv_count, head_size, wide), f32),
            ((2, kv_count, wide), f32),
            ((back * tok_dev, tok_dev), f32),
        ],
        [
            doc_lengths,
            queries,
            key_heads,
            value_heads,
            upper_cotangent,
            readout,
            base_value.reshape(1, tok_dev),
            source_index,
            old_values.reshape(1, tok_dev),
            returns.reshape(1, tok_dev),
        ],
        room,
        2 * unit,
        in_specs=[hbm] * 10,
        scratch_shapes=[
            pltpu.SMEM(doc_lengths.shape, jnp.int32),
            pltpu.SemaphoreType.DMA((10,)),
        ],
    )
    query_here, key_here, value_here, upper_here, readout_here, base_here = outs[:6]
    source_here, old_here, return_here = outs[6:9]
    turned_query, own_raised, own_sum, own_stat, bias = outs[9:]
    if not relay:
        row_args = [old_here] + [rows[0] for rows in seen]
        row_args += [return_here] + [rows[1] for rows in seen]
    (now,) = call(
        functools.partial(source_kernel, seq_count, relay),
        [((2, tok_dev), f32)],
        [source_here, *row_args],
        8,
    )
    bit = seq_count // 2
    size = head_count // 2
    outs = call(
        functools.partial(forward_kernel, back, kv_count, relay, bit),
        [
            ((2, tok_dev), f32),
            ((kv_count, back * tok_dev, wide), f32),
            ((kv_count, head_size, wide), bf16),
            ((2, kv_count, wide), f32),
            (key_heads.shape, bf16),
            ((size, head_size), f32),
            ((size, head_size), f32),
        ],
        [bias, now, base_here, readout_here, turned_query, own_sum, own_stat] + keys + vals,
        room,
        2 * back * unit,
        scratch_shapes=[pltpu.VMEM((head_count, head_size), f32)],
    )
    rows, raised, out, norm, near, keep, away = outs
    keys = [near] + keys[1 + relay :]
    far = swap(away, bit)
    half = kv_count // 2
    splits = [range(0, half), range(half, kv_count)]

    def backward(section, earlier):
        groups = splits[section]
        count = len(groups)
        width = 2 * (kv_width if earlier else count * head_size)
        outs = call(
            functools.partial(backward_kernel, back, kv_count, groups),
            [
                ((count, wide), f32),
                ((count, wide, head_size), bf16),
                ((count, head_size, wide), bf16),
                ((count, back * tok_dev, wide), bf16),
            ]
            + [((tok_dev, width), bf16)] * back,
            [rows, upper_here, readout_here, raised, norm, out, query_here] + vals + earlier,
            room,
            3 * back * unit * count // kv_count,
        )
        return outs[:4], outs[4:]

    first_terms, grads = backward(0, [])
    while bit > 1:
        bit, size = bit // 2, size // 2
        keep, away = call(
            functools.partial(halve_kernel, bit),
            [((size, head_size), f32)] * 2,
            [keep, far],
            scratch_shapes=[pltpu.VMEM((2 * size, head_size), f32)],
        )
        far = swap(away, bit)
    second_terms, grads = backward(1, list(grads))
    returned = [rotate(grads[step - 1], -step) for step in range(1, back + 1)]

    def spread(left, right, bit):
        (total,) = call(sum_kernel, [((own_heads, head_size), f32)], [left, right])
        return total, swap(total, bit, "dp")

    def query_part(section, groups, base):
        args = [own_raised, norm, *(first_terms, second_terms)[section], query_here, key_here]
        args += keys + [value_here]
        aliases = {} if base is None else {len(args): 0}
        specs = [vmem] * len(args) + [hbm] * len(aliases)
        args += [] if base is None else [base]
        width = len(groups) * head_size
        return call(
            functools.partial(query_grad_kernel, back, kv_count, groups),
            [(queries.shape, bf16), ((tok_dev, width), f32), ((tok_dev, width), f32)],
            args,
            room,
            (4 + back) * unit * len(groups) // kv_count,
            in_specs=specs,
            out_specs=[hbm, vmem, vmem],
            scratch_shapes=[
                pltpu.VMEM((len(groups), tok_dev, per_group * head_size), bf16),
                pltpu.SemaphoreType.DMA((len(groups),)),
            ],
            input_output_aliases=aliases,
        )

    own_parts, grad_queries = [], None
    keep, far = spread(keep, far, 1)
    for at in range(1, dp_count.bit_length() - 1):
        keep, far = spread(keep, far, 1 << at)
        if at <= len(splits):
            grad_queries, *parts = query_part(at - 1, splits[at - 1], grad_queries)
            own_parts += parts
    new_values, grad_key_heads, grad_value_heads, grad_readout = call(
        functools.partial(combine_kernel, len(splits)),
        [small, (key_heads.shape, bf16), (key_heads.shape, bf16), ((own_heads, own_size), f32)],
        own_parts + [rows, keep, far] + returned,
        8,
        unit // 100,
    )
    return (
        new_values.reshape(tok_dev),
        grad_queries,
        grad_key_heads,
        grad_value_heads,
        grad_readout,
    )


def solution(mesh):
    return jax.shard_map(
        on_device,
        mesh=mesh,
        in_specs=(
            P(("dp", "seq"), None),
            P(("dp", "seq"), None),
            P(("dp", "seq"), None),
            P(("dp", "seq"), None),
            P(),
            P(("dp", "seq")),
            P(("dp", "seq")),
            P(("dp", "seq")),
            P("dp", None),
            P("dp", None),
        ),
        out_specs=(
            P(("dp", "seq")),
            P(("dp", "seq"), None),
            P(("dp", "seq"), None),
            P(("dp", "seq"), None),
            P("seq", "dp"),
        ),
        check_vma=False,
    )
```
